32 devices in a mesh: groups: 2 (over y), lon: 16 (over z, x, core).
Axes of the slice: x: 2, y: 2, z: 4, core: 2. Of those that a mesh axis runs over, the one named last changes fastest.
Arguments:
- tokens: bfloat16 [8, 24, 96, 512], P('groups', None, 'lon'), parts along dimension 0, may hold values from -6 to 6
- window_shift: int32 [2, 3], replicated, may hold values from 0 to 11, as said below
- fine_gain: float32 [512], replicated, may hold values from 0.25 to 1.75
- fine_qkv: bfloat16 [512, 1536], replicated
- fine_proj: bfloat16 [512, 512], replicated, may hold values from -0.25 to 0.25
- merge_gain: float32 [2048], replicated, may hold values from 0.25 to 1.75
- merge_weight: bfloat16 [2048, 512], replicated, may hold values from -0.125 to 0.125
- coarse_gain: float32 [512], replicated, may hold values from 0.25 to 1.75
- coarse_qkv: bfloat16 [512, 1536], replicated
- coarse_proj: bfloat16 [512, 512], replicated, may hold values from -0.25 to 0.25
- expand_weight: bfloat16 [512, 2048], replicated, may hold values from -0.25 to 0.25
- expand_gain: float32 [512], replicated, may hold values from 0.25 to 1.75
Outputs:
- forecast_state: bfloat16 [8, 24, 96, 512], P('groups', None, 'lon'), parts along dimension 0
The draws below stay inside these ranges and needn't reach their ends.
There are 2 independent parts, one for each index of `groups`. The reference program is written for one: setup_inputs(seed, part) draws one part's arguments, and reference() takes and returns one part's arrays. A program takes and returns all parts, laid end to end along the dimension named above; an argument that names none is the same for every part. Nothing has to cross between parts.
Inputs may be any that keep to these rules, and one draw needn't show every extreme that they name: window_shift[k] holds offsets 0 to 1, 0 to 5 and 0 to 11 along level, latitude and longitude.
All inputs are finite; a program needn't handle non-finite values.
Results may differ from the reference program's by a relative error of at most 0.013.
Values may be sent and summed in bfloat16 or wider, within the bound.
No kernel may reach another device: no remote copies, remote signals or barrier semaphores. Data moves between devices by JAX's collectives and lax.ppermute only.
A program may use at most 128 MiB of HBM per device.

```python
import math
import jax
import jax.numpy as jnp
from jax import lax

LEV = 4
LAT = 24
LON_DEV = 6
D = 512
HEADS = 8
DC = 512
HC = 8
WIN_LEV = 2
WIN_LAT = 6
WIN_LON = 12
LON = 96


def projection_draw(key, features):
    base = jax.random.normal(key, (features, 3 * features), jnp.float32) * features ** (-0.5)
    return base.astype(jnp.bfloat16)


def draw_fine_qkv(key, part):
    return projection_draw(jax.random.fold_in(key, 11), D)


def draw_coarse_qkv(key, part):
    return projection_draw(jax.random.fold_in(key, 23), DC)


def draw_window_shift(key, part):
    limits = jnp.array([WIN_LEV, WIN_LAT, WIN_LON], dtype=jnp.int32)
    offsets = jax.random.randint(jax.random.fold_in(key, 37), (2, 3), 0, limits, dtype=jnp.int32)
    chosen = jax.random.randint(jax.random.fold_in(key, 41), (), 0, 2, dtype=jnp.int32)
    row_ids = jnp.arange(2, dtype=jnp.int32)
    lon_col = jnp.where(row_ids == chosen, WIN_LON - 1, offsets[:, 2])
    lev_col = jnp.where(row_ids == chosen, offsets[:, 0], 0)
    offsets = offsets.at[:, 2].set(lon_col)
    offsets = offsets.at[:, 0].set(lev_col)
    return offsets.astype(jnp.int32)


def block_scale(rng, shape, pieces, smallest, top_value):
    def one(dim, shards_of):
        steps = jax.random.uniform(jax.random.fold_in(jax.random.fold_in(rng, 6), dim), (shards_of,), jnp.float32, smallest / len(pieces), top_value / len(pieces))
        return jnp.repeat(jnp.exp(steps), shape[dim] // shards_of).reshape((-1,) + (1,) * (len(shape) - dim - 1))

    level = one(*pieces[0])
    for cut in pieces[1:]:
        level = level * one(*cut)
    return level


def gaussian(rng, shape, scale, bound, shards=(), kind=jnp.bfloat16):
    level = block_scale(rng, shape, shards, -0.22, 0.18) if shards else 1.0
    entries = jax.random.normal(rng, shape, jnp.float32) * scale * level
    return jnp.minimum(jnp.maximum(entries, -bound), bound).astype(kind)


def setup_inputs(seed: int = 0, part: int = 0) -> dict:
    key_list = jax.random.split(jax.random.key(seed), 13)
    part_keys = jax.random.split(jax.random.fold_in(key_list[12], part), 13)
    tokens = gaussian(part_keys[0], (LEV, LAT, LON, D), 1.0, 6.0, ((2, 16),))
    window_shift = draw_window_shift(jax.random.fold_in(key_list[12], 71), part)
    fine_gain = jnp.clip(1.0 + 0.15 * jax.random.normal(key_list[2], (D,), jnp.float32), 0.25, 1.75)
    fine_qkv = draw_fine_qkv(jax.random.fold_in(key_list[12], 71), part)
    fine_proj = gaussian(key_list[4], (D, D), D ** -0.5, 0.25)
    merge_gain = jnp.clip(1.0 + 0.15 * jax.random.normal(key_list[5], (4 * D,), jnp.float32), 0.25, 1.75)
    merge_weight = gaussian(key_list[6], (4 * D, DC), (4 * D) ** -0.5, 0.125)
    coarse_gain = jnp.clip(1.0 + 0.15 * jax.random.normal(key_list[7], (DC,), jnp.float32), 0.25, 1.75)
    coarse_qkv = draw_coarse_qkv(jax.random.fold_in(key_list[12], 71), part)
    coarse_proj = gaussian(key_list[9], (DC, DC), DC ** -0.5, 0.25)
    expand_weight = gaussian(key_list[10], (DC, 4 * D), DC ** -0.5, 0.25)
    expand_gain = jnp.clip(1.0 + 0.15 * jax.random.normal(key_list[11], (D,), jnp.float32), 0.25, 1.75)
    return dict(tokens=tokens, window_shift=window_shift, fine_gain=fine_gain, fine_qkv=fine_qkv, fine_proj=fine_proj, merge_gain=merge_gain, merge_weight=merge_weight, coarse_gain=coarse_gain, coarse_qkv=coarse_qkv, coarse_proj=coarse_proj, expand_weight=expand_weight, expand_gain=expand_gain)


EPSILON = 1e-05

def layer_norm(inputs, gain_vec):
    inputs = inputs.astype(jnp.float32)
    center = inputs - lax.optimization_barrier(jnp.mean(inputs, axis=-1, keepdims=True))
    spread = lax.optimization_barrier(jnp.mean(center * center, axis=-1, keepdims=True))
    return center * lax.rsqrt(spread + EPSILON) * gain_vec

def rolled_ids(length, offset, extent):
    placed = jnp.arange(length, dtype=jnp.int32)
    source = (placed - offset) % length
    return (source + offset) // extent

def roll_grid(tensor_in, offsets, factor):
    return jnp.roll(jnp.roll(tensor_in, factor * offsets[0], 0), factor * offsets[1], 1)

def window_attention(queries, key_block, value_block, query_cols, key_cols, offsets, lon_total, head_count):
    levels, lat_rows, query_wide, features = queries.shape
    key_wide = key_block.shape[2]
    head_size = features // head_count
    lev_blocks = levels // WIN_LEV
    lat_blocks = lat_rows // WIN_LAT

    def blocked(tensor_in, wide_cols):
        tensor_in = tensor_in.reshape(lev_blocks, WIN_LEV, lat_blocks, WIN_LAT, wide_cols, head_count, head_size)
        tensor_in = tensor_in.transpose(0, 2, 1, 3, 4, 5, 6)
        return tensor_in.reshape(lev_blocks * lat_blocks, WIN_LEV * WIN_LAT * wide_cols, head_count, head_size)
    lev_ids = rolled_ids(levels, offsets[0], WIN_LEV).reshape(lev_blocks, WIN_LEV)
    row_ids = rolled_ids(lat_rows, offsets[1], WIN_LAT).reshape(lat_blocks, WIN_LAT)
    lev_same = lev_ids[:, :, None] == lev_ids[:, None, :]
    row_same = row_ids[:, :, None] == row_ids[:, None, :]
    query_win = (query_cols + offsets[2]) % lon_total // WIN_LON
    key_win = (key_cols + offsets[2]) % lon_total // WIN_LON
    col_same = query_win[:, None] == key_win[None, :]
    allowed = lev_same[:, None, :, None, None, :, None, None] & row_same[None, :, None, :, None, None, :, None] & col_same[None, None, None, None, :, None, None, :]
    allowed = allowed.reshape(lev_blocks * lat_blocks, WIN_LEV * WIN_LAT * query_wide, WIN_LEV * WIN_LAT * key_wide)
    query_b = blocked(queries, query_wide).astype(jnp.float32)
    key_b = blocked(key_block, key_wide).astype(jnp.float32)
    value_b = blocked(value_block, key_wide).astype(jnp.float32)
    scores = jnp.einsum('bqhd,bkhd->bhqk', query_b, key_b) / math.sqrt(head_size)
    scores = jnp.where(allowed[:, None], scores, -1e+30)
    row_max = lax.optimization_barrier(jnp.max(scores, axis=-1, keepdims=True))
    expo = jnp.exp(scores - row_max)
    weight = (expo / lax.optimization_barrier(jnp.sum(expo, axis=-1, keepdims=True))).astype(jnp.bfloat16)
    mixture = jnp.einsum('bhqk,bkhd->bqhd', weight.astype(jnp.float32), value_b).astype(jnp.bfloat16)
    mixture = mixture.reshape(lev_blocks, lat_blocks, WIN_LEV, WIN_LAT, query_wide, features)
    return mixture.transpose(0, 2, 1, 3, 4, 5).reshape(levels, lat_rows, query_wide, features)

def attention_block(grid, gain_vec, qkv_weight, proj_weight, offsets, head_count, block_cols):
    levels, lat_rows, lon_total, features = grid.shape
    reach = WIN_LON - 1
    normed = layer_norm(grid, gain_vec).astype(jnp.bfloat16)
    projected = jnp.dot(normed, qkv_weight, preferred_element_type=jnp.float32).astype(jnp.bfloat16)
    queries = roll_grid(projected[..., :features], offsets, 1)
    key_block = roll_grid(projected[..., features:2 * features], offsets, 1)
    value_block = roll_grid(projected[..., 2 * features:], offsets, 1)

    def one_block(index):
        first_col = index * block_cols
        query_cols = first_col + jnp.arange(block_cols, dtype=jnp.int32)
        key_cols = (first_col - reach + jnp.arange(block_cols + 2 * reach, dtype=jnp.int32)) % lon_total
        query_part = lax.dynamic_slice_in_dim(queries, first_col, block_cols, 2)
        key_part = jnp.take(key_block, key_cols, axis=2)
        value_part = jnp.take(value_block, key_cols, axis=2)
        return window_attention(query_part, key_part, value_part, query_cols, key_cols, offsets, lon_total, head_count)
    outputs = lax.map(one_block, jnp.arange(lon_total // block_cols, dtype=jnp.int32))
    outputs = outputs.transpose(1, 2, 0, 3, 4).reshape(levels, lat_rows, lon_total, features)
    outputs = roll_grid(outputs, offsets, -1)
    update = jnp.dot(outputs, proj_weight, preferred_element_type=jnp.float32)
    return (grid.astype(jnp.float32) + update).astype(jnp.bfloat16)

def merge_patches(fine, gain_vec, weight):
    levels, lat_rows, lon_cols, features = fine.shape
    grouped = fine.reshape(levels, lat_rows // 2, 2, lon_cols // 2, 2, features)
    grouped = grouped.transpose(0, 1, 3, 4, 2, 5).reshape(levels, lat_rows // 2, lon_cols // 2, 4 * features)
    merged = layer_norm(grouped, gain_vec).astype(jnp.bfloat16)
    return jnp.dot(merged, weight, preferred_element_type=jnp.float32).astype(jnp.bfloat16)

def expand_patches(coarse, weight, gain_vec, fine):
    levels, lat_rows, lon_cols, channels = coarse.shape
    features = fine.shape[-1]
    expanded = jnp.dot(coarse, weight, preferred_element_type=jnp.float32)
    expanded = layer_norm(expanded.reshape(levels, lat_rows, lon_cols, 2, 2, features), gain_vec)
    expanded = expanded.transpose(0, 1, 4, 2, 3, 5).reshape(levels, 2 * lat_rows, 2 * lon_cols, features)
    return (fine.astype(jnp.float32) + expanded).astype(jnp.bfloat16)

def reference(tokens, window_shift, fine_gain, fine_qkv, fine_proj, merge_gain, merge_weight, coarse_gain, coarse_qkv, coarse_proj, expand_weight, expand_gain):
    fine = attention_block(tokens, fine_gain, fine_qkv, fine_proj, window_shift[0], HEADS, LON_DEV)
    coarse = merge_patches(fine, merge_gain, merge_weight)
    coarse = attention_block(coarse, coarse_gain, coarse_qkv, coarse_proj, window_shift[1], HC, LON_DEV // 2)
    return expand_patches(coarse, expand_weight, expand_gain, fine)
```

```python
import functools

import jax
import jax.numpy as jnp
from jax import lax
from jax.experimental import pallas as pl
from jax.experimental.pallas import tpu as pltpu
from jax.sharding import PartitionSpec as P

HEADS = 8
HC = 8
WIN_LEV = 2
WIN_LAT = 6
WIN_LON = 12
EPSILON = 1e-05
NEG = -1e30
F32 = jnp.float32
BF16 = jnp.bfloat16


def permuted(value, steps):
    count = lax.axis_size("lon")
    return lax.ppermute(value, "lon", [(s, (s + steps) % count) for s in range(count)])


def swapped(value):
    count = lax.axis_size("lon")
    return lax.ppermute(value, "lon", [(s, s ^ 1) for s in range(count)])


def layer_norm(x, gain):
    center = x - jnp.mean(x, axis=-1, keepdims=True)
    spread = jnp.mean(center * center, axis=-1, keepdims=True)
    return center * lax.rsqrt(spread + EPSILON) * gain


def dot(a, b):
    return jnp.dot(a, b, preferred_element_type=F32)


def dot_t(a, b):
    return lax.dot_general(a, b, (((1,), (1,)), ((), ())), preferred_element_type=F32)


def level_of(core, slot, a):
    if slot == 0:
        return 2 * core
    return jnp.where(core == 0, 1 + 2 * a, 3 - 2 * a)


def iota(shape, axis):
    return lax.broadcasted_iota(jnp.int32, shape, axis)


def take(ref, start, count, stride=1):
    at = pl.ds(start, count, stride=stride) if stride > 1 else pl.ds(start, count)
    return jnp.concatenate([ref[k, at, :] for k in range(ref.shape[0])], axis=1)


def put(ref, start, value, stride=1):
    at = pl.ds(start, value.shape[0], stride=stride) if stride > 1 else pl.ds(start, value.shape[0])
    for k in range(ref.shape[0]):
        ref[k, at, :] = value[:, k * 128 : (k + 1) * 128]


def chunked(count, width):
    return pltpu.VMEM((width // 128, count, 128), F32)


def split_kernel(shift_ref, tok_ref, keep_ref, send_ref, scr):
    core = lax.axis_index("lon") % 2
    levels, rows, cols, feats = tok_ref.shape
    a, b = shift_ref[0, 0], shift_ref[0, 1]
    for target, out_ref in ((core, keep_ref), (1 - core, send_ref)):
        for slot in range(2):
            level = level_of(target, slot, a)
            for placed in range(rows):
                source = placed - b
                source = jnp.where(source < 0, source + rows, source)
                put(scr, (placed * 2 + slot) * 8, tok_ref[level, source].astype(F32))
        for col in range(cols):
            out_ref[col] = take(scr, col, rows * 2, 8).astype(BF16)


def head_pair(q, keys, values, picks, bias, scale):
    size = q.shape[0]
    low = iota(q.shape, 1) < q.shape[1] // 2
    zero = jnp.zeros_like(q)
    q2 = jnp.concatenate([jnp.where(low, q, zero), jnp.where(low, zero, q)], axis=0)
    if picks is None:
        scores = dot_t(q2, keys[0])
    else:
        scores = jnp.where(picks, dot_t(q2, keys[0]), dot_t(q2, keys[1]))
    scores = scores + bias
    top = jnp.max(scores, axis=-1, keepdims=True)
    expo = jnp.exp((scores - top) * scale)
    total = jnp.sum(expo, axis=-1, keepdims=True)
    if picks is None:
        mixed = dot(expo.astype(BF16), values[0])
    else:
        none = jnp.zeros_like(expo)
        mixed = dot(jnp.where(picks, expo, none).astype(BF16), values[0]) + dot(
            jnp.where(picks, none, expo).astype(BF16), values[1]
        )
    mixed = mixed / total
    return jnp.where(low, mixed[:size], mixed[size:])


def fine_kernel(
    shift_ref, x_ref, r_ref, gain_ref, qkv_ref, proj_ref, mgain_ref, mw_ref,
    keep_ref, send_ref, coarse_ref,
    xs, rs, qkv, kvr, mix, fu, scr, bias,
):
    core = lax.axis_index("lon") % 2
    cols, depth, feats = x_ref.shape
    rows = depth // 2
    wins = rows // WIN_LAT
    size = WIN_LAT * 2 * cols
    a, b, c = shift_ref[0, 0], shift_ref[0, 1], shift_ref[0, 2]
    for col in range(cols):
        put(xs, col, x_ref[col].astype(F32), cols)
        put(rs, col, r_ref[col].astype(F32), cols)
    gain = gain_ref[...]
    for j in range(wins):
        at = pl.ds(j * size, size)
        normed = layer_norm(take(xs, j * size, size), gain).astype(BF16)
        qkv[at, :] = dot(normed, qkv_ref[...]).astype(BF16)
        normed = layer_norm(take(rs, j * size, size), gain).astype(BF16)
        kvr[at, :] = dot(normed, qkv_ref[:, feats:]).astype(BF16)

    def parts(shape, axis):
        index = iota(shape, axis) % size
        return index // (2 * cols), (index // cols) % 2, index % cols

    full = (2 * size, size)
    q_row, q_slot, q_col = parts(full, 0)
    k_row, k_slot, k_col = parts(full, 1)
    picks = (q_col + c >= cols) == (k_col + c >= cols)
    levels_ok = (q_slot == k_slot) | (a == 0) | (core == 1)
    rows_ok = (q_row < b) == (k_row < b)
    bias[0] = jnp.where(levels_ok & rows_ok, 0.0, NEG)
    bias[1] = jnp.where(levels_ok, 0.0, NEG)
    scale = (feats // HEADS) ** -0.5
    for j in range(wins):
        at = pl.ds(j * size, size)
        for pair in range(feats // 128):
            lanes = pl.ds(pair * 128, 128)
            k_lanes = pl.ds(feats + pair * 128, 128)
            v_lanes = pl.ds(2 * feats + pair * 128, 128)
            mix[at, lanes] = head_pair(
                qkv[at, lanes],
                (qkv[at, k_lanes], kvr[at, lanes]),
                (qkv[at, v_lanes], kvr[at, k_lanes]),
                picks,
                bias[min(j, 1)],
                scale,
            ).astype(BF16)
    half = rows // 2
    unit = 2 * cols
    for j in range(wins):
        at = pl.ds(j * size, size)
        fine = take(xs, j * size, size) + dot(mix[at, :], proj_ref[...])
        fine = fine.astype(BF16).astype(F32)
        for inner in range(WIN_LAT):
            source = j * WIN_LAT + inner - b
            source = jnp.where(source < 0, source + rows, source)
            start = (source % 2) * (half * unit) + (source // 2) * unit
            put(fu, pl.multiple_of(start, 8), fine[inner * unit : (inner + 1) * unit])
    own_cols = cols // 2
    for target, out_ref in ((core, keep_ref), (1 - core, send_ref)):
        for col in range(own_cols):
            put(scr, col, take(fu, target * own_cols + col, depth, cols), 8)
        packed = take(scr, 0, depth * 8).reshape(depth, 8, feats)
        out_ref[...] = packed[:, :own_cols, :].astype(BF16)
    pieces = []
    count = half * unit // 2
    for q in range(2):
        for p in range(2):
            pieces.append(take(fu, p * half * unit + q, count, 2))
    width = 4 * feats
    mean = sum(jnp.sum(piece, axis=-1, keepdims=True) for piece in pieces) / width
    pieces = [piece - mean for piece in pieces]
    spread = sum(jnp.sum(piece * piece, axis=-1, keepdims=True) for piece in pieces) / width
    scaling = lax.rsqrt(spread + EPSILON)
    total = jnp.zeros((count, mw_ref.shape[1]), F32)
    for k, piece in enumerate(pieces):
        merged = (piece * scaling * mgain_ref[k : k + 1, :]).astype(BF16)
        total = total + dot(merged, mw_ref[k * feats : (k + 1) * feats, :])
    coarse_ref[...] = total.astype(BF16)


def coarse_kernel(
    shift_ref, own_ref, l1_ref, r1_ref, l2_ref, r2_ref, gain_ref, qkv_ref, proj_ref,
    out_ref, keys, values, bias, mix, *, own_cols,
):
    place = lax.axis_index("lon")
    core = place % 2
    chips_wide = WIN_LON // own_cols
    side = (place // 2) % chips_wide
    size, feats = own_ref.shape
    a, b, c = shift_ref[1, 0], shift_ref[1, 1], shift_ref[1, 2]
    gain = gain_ref[...]
    refs = (own_ref, l1_ref, r1_ref, l2_ref, r2_ref)
    offsets = (0, -1, 1, -2, 2)
    queries = None
    for n, ref in enumerate(refs):
        at = pl.ds(n * size, size)
        normed = layer_norm(ref[...].astype(F32), gain).astype(BF16)
        if n == 0:
            queries = dot(normed, qkv_ref[:, :feats]).astype(BF16)
        keys[at, :] = dot(normed, qkv_ref[:, feats : 2 * feats]).astype(BF16)
        values[at, :] = dot(normed, qkv_ref[:, 2 * feats :]).astype(BF16)

    def ids(index, offset):
        row = index // (2 * own_cols)
        slot = (index // own_cols) % 2
        col = (side + offset + chips_wide) * own_cols + index % own_cols
        window = (col + c) // WIN_LON
        return ((row + b) // WIN_LAT) * 2 + jnp.where((a == 0) | (core == 1), 0, slot), window

    shape = (2 * size, size)
    q_id, q_win = ids(iota(shape, 0) % size, 0)
    for n, offset in enumerate(offsets):
        k_id, k_win = ids(iota(shape, 1), offset)
        bias[:, n * size : (n + 1) * size] = jnp.where((q_id == k_id) & (q_win == k_win), 0.0, NEG)
    scale = (feats // HC) ** -0.5
    for pair in range(feats // 128):
        lanes = pl.ds(pair * 128, 128)
        mix[:, lanes] = head_pair(
            queries[:, pair * 128 : (pair + 1) * 128],
            (keys[:, lanes],),
            (values[:, lanes],),
            None,
            bias[...],
            scale,
        ).astype(BF16)
    out = own_ref[...].astype(F32) + dot(mix[...], proj_ref[...])
    out_ref[...] = out.astype(BF16)


def expand_kernel(
    shift_ref, own_ref, other_ref, fkeep_ref, fother_ref, gain_ref, weight_ref,
    out_ref, cs, ex, *, own_cols,
):
    core = lax.axis_index("lon") % 2
    size, feats = own_ref.shape
    units = size // own_cols
    home = own_cols // 2
    a1, a2 = shift_ref[0, 0], shift_ref[1, 0]
    crossed = jnp.where(a1 == a2, 0, 1)
    put(cs.at[0], 0, own_ref[...].astype(F32))
    put(cs.at[1], 0, other_ref[...].astype(F32))
    blocks = []
    for which in range(2):
        for col in range(home):
            blocks.append(take(cs.at[which], core * home + col, units, own_cols))
    blocks = jnp.concatenate(blocks, axis=0).astype(BF16)
    gain = gain_ref[...]
    for q in range(2):
        for p in range(2):
            k = 2 * q + p
            piece = layer_norm(dot(blocks, weight_ref[:, k * feats : (k + 1) * feats]), gain)
            for which in range(2):
                for col in range(home):
                    first = (which * home + col) * units
                    put(ex.at[which], p * 8 + 2 * col + q, piece[first : first + units], 16)
    half = units // 2
    for which, (target, f_ref) in enumerate(((core, fkeep_ref), (1 - core, fother_ref))):
        for slot in range(2):
            level = level_of(target, slot, a1)
            source = which if slot == 0 else jnp.where(crossed == 1, 1 - which, which)
            for i in range(half):
                for p in range(2):
                    add = take(ex.at[source], (i * 2 + slot) * 16 + p * 8, 2 * home)
                    fine = f_ref[(p * half + i) * 2 + slot].astype(F32)
                    out_ref[level, 2 * i + p] = (fine + add).astype(BF16)


VMEM_SPEC = pl.BlockSpec(memory_space=pltpu.VMEM)
SMEM_SPEC = pl.BlockSpec(memory_space=pltpu.SMEM)


def call(kernel, name, outs, scratch, arrays, cost=None):
    return pl.pallas_call(
        kernel,
        name=name,
        out_shape=outs,
        in_specs=[SMEM_SPEC] + [VMEM_SPEC] * (len(arrays) - 1),
        out_specs=jax.tree.map(lambda _: VMEM_SPEC, outs),
        scratch_shapes=scratch,
        cost_estimate=cost,
    )(*arrays)


def local(
    tokens,
    window_shift,
    fine_gain,
    fine_qkv,
    fine_proj,
    merge_gain,
    merge_weight,
    coarse_gain,
    coarse_qkv,
    coarse_proj,
    expand_weight,
    expand_gain,
):
    levels, rows, dev_cols, feats = tokens.shape
    cols = 2 * dev_cols
    depth = 2 * rows
    assert levels == 4 and cols == WIN_LON and rows % (2 * WIN_LAT) == 0
    core = lax.axis_index("lon") % 2
    sds = jax.ShapeDtypeStruct
    half = sds((dev_cols, depth, feats), BF16)
    keep, send = call(
        split_kernel, "split", (half, half), [chunked(depth * 8, feats)],
        (window_shift, tokens),
    )
    other = swapped(send)
    grid = jnp.concatenate(
        [jnp.where(core == 0, keep, other), jnp.where(core == 0, other, keep)], axis=0
    )

    def branch(c):
        def run(grid):
            if c == 0:
                return grid
            left = permuted(grid[: cols - c], -2)
            right = permuted(grid[cols - c :], 2)
            return jnp.concatenate([left, right], axis=0)

        return run

    around = lax.switch(window_shift[0, 2], [branch(c) for c in range(WIN_LON)], grid)
    tokens_n = depth * cols
    size = WIN_LAT * 2 * cols
    coarse_n = tokens_n // 4
    channels = merge_weight.shape[1]
    fine_half = sds((depth, dev_cols, feats), BF16)
    fine_keep, fine_send, coarse = call(
        fine_kernel, "fine", (fine_half, fine_half, sds((coarse_n, channels), BF16)),
        [
            chunked(tokens_n, feats),
            chunked(tokens_n, feats),
            pltpu.VMEM((tokens_n, 3 * feats), BF16),
            pltpu.VMEM((tokens_n, 2 * feats), BF16),
            pltpu.VMEM((tokens_n, feats), BF16),
            chunked(tokens_n, feats),
            chunked(depth * 8, feats),
            pltpu.VMEM((2, 2 * size, size), F32),
        ],
        (
            window_shift, grid, around, fine_gain.reshape(1, feats), fine_qkv, fine_proj,
            merge_gain.reshape(4, feats), merge_weight,
        ),
    )
    fine_other = swapped(fine_send)
    coarse_cols = dev_cols
    slot = (jnp.arange(coarse_n, dtype=jnp.int32) // coarse_cols) % 2
    crossed = window_shift[0, 0] != window_shift[1, 0]
    coarse = jnp.where((slot[:, None] == 1) & crossed, swapped(coarse), coarse)
    l1, r1 = permuted(coarse, 2), permuted(coarse, -2)
    l2, r2 = permuted(coarse, 4), permuted(coarse, -4)
    coarse_out = call(
        functools.partial(coarse_kernel, own_cols=coarse_cols), "coarse",
        sds((coarse_n, channels), BF16),
        [
            pltpu.VMEM((5 * coarse_n, channels), BF16),
            pltpu.VMEM((5 * coarse_n, channels), BF16),
            pltpu.VMEM((2 * coarse_n, 5 * coarse_n), F32),
            pltpu.VMEM((coarse_n, channels), BF16),
        ],
        (
            window_shift, coarse, l1, r1, l2, r2, coarse_gain.reshape(1, channels), coarse_qkv,
            coarse_proj,
        ),
    )
    coarse_other = swapped(coarse_out)
    return call(
        functools.partial(expand_kernel, own_cols=coarse_cols), "expand",
        sds(tokens.shape, BF16),
        [
            pltpu.VMEM((2, channels // 128, coarse_n, 128), F32),
            pltpu.VMEM((2, feats // 128, depth // 2 * 16, 128), F32),
        ],
        (
            window_shift, coarse_out, coarse_other, fine_keep, fine_other,
            expand_gain.reshape(1, feats), expand_weight,
        ),
    )


def solution(mesh):
    placed = (P("groups", None, "lon", None), P(), P(), P(), P(), P(), P(), P(), P(), P(), P(), P())
    return jax.shard_map(
        local, mesh=mesh, in_specs=placed, out_specs=P("groups", None, "lon", None), check_vma=False
    )
```

```python
import functools

import jax
import jax.numpy as jnp
from jax import lax
from jax.experimental import pallas as pl
from jax.experimental.pallas import tpu as pltpu
from jax.sharding import PartitionSpec as P

HEADS = 8
HC = 8
WIN_LEV = 2
WIN_LAT = 6
WIN_LON = 12
EPSILON = 1e-05
NEG = -1e30
FINE_MIB = 28
COARSE_MIB = 16
EXPAND_MIB = 16
F32 = jnp.float32
BF16 = jnp.bfloat16


def permuted(value, steps):
    count = lax.axis_size("lon")
    return lax.ppermute(value, "lon", [(s, (s + steps) % count) for s in range(count)])


def swapped(value):
    count = lax.axis_size("lon")
    return lax.ppermute(value, "lon", [(s, s ^ 1) for s in range(count)])


def layer_norm(x, gain):
    center = x - jnp.mean(x, axis=-1, keepdims=True)
    spread = jnp.mean(center * center, axis=-1, keepdims=True)
    return center * lax.rsqrt(spread + EPSILON) * gain


def dot(a, b):
    return jnp.dot(a, b, preferred_element_type=F32)


def dot_t(a, b):
    return lax.dot_general(a, b, (((1,), (1,)), ((), ())), preferred_element_type=F32)


def level_of(core, slot, a):
    if slot == 0:
        return 2 * core
    return jnp.where(core == 0, 1 + 2 * a, 3 - 2 * a)


def iota(shape, axis):
    return lax.broadcasted_iota(jnp.int32, shape, axis)


def take(ref, start, count, stride=1):
    at = pl.ds(start, count, stride=stride) if stride > 1 else pl.ds(start, count)
    return jnp.concatenate([ref[k, at, :] for k in range(ref.shape[0])], axis=1)


def put(ref, start, value, stride=1):
    at = pl.ds(start, value.shape[0], stride=stride) if stride > 1 else pl.ds(start, value.shape[0])
    for k in range(ref.shape[0]):
        ref[k, at, :] = value[:, k * 128 : (k + 1) * 128]


def chunked(count, width):
    return pltpu.VMEM((width // 128, count, 128), F32)


def head_pair(q, keys, values, picks, bias, scale):
    size = q.shape[0]
    low = iota(q.shape, 1) < q.shape[1] // 2
    zero = jnp.zeros_like(q)
    q2 = jnp.concatenate([jnp.where(low, q, zero), jnp.where(low, zero, q)], axis=0)
    if picks is None:
        scores = dot_t(q2, keys[0])
    else:
        scores = jnp.where(picks, dot_t(q2, keys[0]), dot_t(q2, keys[1]))
    scores = scores + bias
    top = jnp.max(scores, axis=-1, keepdims=True)
    expo = jnp.exp((scores - top) * scale)
    total = jnp.sum(expo, axis=-1, keepdims=True)
    if picks is None:
        mixed = dot(expo.astype(BF16), values[0])
    else:
        none = jnp.zeros_like(expo)
        mixed = dot(jnp.where(picks, expo, none).astype(BF16), values[0]) + dot(
            jnp.where(picks, none, expo).astype(BF16), values[1]
        )
    mixed = mixed / total
    return jnp.where(low, mixed[:size], mixed[size:])


def fine_kernel(
    shift_ref, x_ref, r_ref, gain_ref, qkv_ref, proj_ref, mgain_ref, mw_ref,
    keep_ref, send_ref, coarse_ref,
    xs, rs, qkv, kvr, mix, fr, fu, bias,
):
    core = lax.axis_index("lon") % 2
    cols, slots, rows, feats = x_ref.shape
    unit = slots * cols
    wins = rows // WIN_LAT
    size = WIN_LAT * unit
    a, b, c = shift_ref[0, 0], shift_ref[0, 1], shift_ref[0, 2]
    for ref, scr in ((x_ref, xs), (r_ref, rs)):
        for col in range(cols):
            for slot in range(slots):
                put(scr, size + slot * cols + col, ref[col, slot].astype(F32), unit)
        put(scr, 0, take(scr, rows * unit, size))
    starts = [pl.multiple_of(((j + 1) * WIN_LAT - b) * unit, 8) for j in range(wins)]
    gain = gain_ref[...]
    for j in range(wins):
        at = pl.ds(j * size, size)
        normed = layer_norm(take(xs, starts[j], size), gain).astype(BF16)
        qkv[at, :] = dot(normed, qkv_ref[...]).astype(BF16)
        normed = layer_norm(take(rs, starts[j], size), gain).astype(BF16)
        kvr[at, :] = dot(normed, qkv_ref[:, feats:]).astype(BF16)

    def parts(index):
        return index // unit, (index // cols) % slots, index % cols

    q_row, q_slot, q_col = parts(iota((2 * size, 1), 0) % size)
    k_row, k_slot, k_col = parts(iota((1, size), 1))
    q_side = jnp.where(q_col + c >= cols, 1, 0)
    k_side = jnp.where(k_col + c >= cols, 1, 0)
    apart = jnp.where((a == 0) | (core == 1), 0, 1)
    q_slot, k_slot = q_slot * apart, k_slot * apart
    q_id = q_slot * 2 + jnp.where(q_row < b, 1, 0)
    k_id = k_slot * 2 + jnp.where(k_row < b, 1, 0)
    bias[0] = jnp.where(q_id == k_id, 0.0, NEG)
    bias[1] = jnp.where(q_slot == k_slot, 0.0, NEG)
    picks = q_side == k_side
    scale = (feats // HEADS) ** -0.5
    for j in range(wins):
        at = pl.ds(j * size, size)
        for pair in range(feats // 128):
            lanes = pl.ds(pair * 128, 128)
            k_lanes = pl.ds(feats + pair * 128, 128)
            v_lanes = pl.ds(2 * feats + pair * 128, 128)
            mix[at, lanes] = head_pair(
                qkv[at, lanes],
                (qkv[at, k_lanes], kvr[at, lanes]),
                (qkv[at, v_lanes], kvr[at, k_lanes]),
                picks,
                bias[min(j, 1)],
                scale,
            ).astype(BF16)
    half = rows // 2
    for j in range(wins):
        at = pl.ds(j * size, size)
        fine = take(xs, starts[j], size) + dot(mix[at, :], proj_ref[...])
        fine = fine.astype(BF16).astype(F32)
        for inner in range(WIN_LAT):
            source = j * WIN_LAT + inner - b
            source = jnp.where(source < 0, source + rows, source)
            put(fr, pl.multiple_of(source * unit, 8), fine[inner * unit : (inner + 1) * unit])
    own_cols = cols // 2
    for slot in range(slots):
        for col in range(own_cols):
            for target, out_ref in ((core, keep_ref), (1 - core, send_ref)):
                start = slot * cols + target * own_cols + col
                out_ref[col, slot] = take(fr, start, rows, unit).astype(BF16)
    for p in range(2):
        for slot in range(slots):
            for col in range(cols):
                first = slot * cols + col
                piece = take(fr, p * unit + first, half, 2 * unit)
                put(fu, (p * slots + slot) * half * cols + col, piece, cols)
    pieces = []
    count = half * unit // 2
    for q in range(2):
        for p in range(2):
            pieces.append(take(fu, p * half * unit + q, count, 2))
    width = 4 * feats
    mean = sum(jnp.sum(piece, axis=-1, keepdims=True) for piece in pieces) / width
    pieces = [piece - mean for piece in pieces]
    spread = sum(jnp.sum(piece * piece, axis=-1, keepdims=True) for piece in pieces) / width
    scaling = lax.rsqrt(spread + EPSILON)
    total = jnp.zeros((count, mw_ref.shape[1]), F32)
    for k, piece in enumerate(pieces):
        lanes = slice(k * feats, (k + 1) * feats)
        merged = (piece * scaling * mgain_ref[:, lanes]).astype(BF16)
        total = total + dot(merged, mw_ref[lanes, :])
    coarse_ref[...] = total.astype(BF16).reshape(coarse_ref.shape)


def coarse_kernel(
    shift_ref, own_ref, l1_ref, r1_ref, l2_ref, r2_ref, gain_ref, qkv_ref, proj_ref,
    out_ref, keys, values, bias, mix, *, own_cols,
):
    place = lax.axis_index("lon")
    core = place % 2
    chips_wide = WIN_LON // own_cols
    side = (place // 2) % chips_wide
    slots, depth, feats = own_ref.shape
    size = slots * depth
    a, b, c = shift_ref[1, 0], shift_ref[1, 1], shift_ref[1, 2]
    gain = gain_ref[...]
    refs = (own_ref, l1_ref, r1_ref, l2_ref, r2_ref)
    offsets = (0, -1, 1, -2, 2)
    queries = None
    for n, ref in enumerate(refs):
        at = pl.ds(n * size, size)
        full = ref[...].astype(F32).reshape(size, feats)
        normed = layer_norm(full, gain).astype(BF16)
        if n == 0:
            queries = dot(normed, qkv_ref[:, :feats]).astype(BF16)
        keys[at, :] = dot(normed, qkv_ref[:, feats : 2 * feats]).astype(BF16)
        values[at, :] = dot(normed, qkv_ref[:, 2 * feats :]).astype(BF16)

    def ids(index, offset):
        slot = index // depth
        row = (index // own_cols) % (depth // own_cols)
        col = (side + offset + chips_wide) * own_cols + index % own_cols
        window = (col + c) // WIN_LON
        apart = jnp.where((a == 0) | (core == 1), 0, slot)
        return (window * 8 + (row + b) // WIN_LAT) * 2 + apart

    q_id = ids(iota((2 * size, 1), 0) % size, 0)
    for n, offset in enumerate(offsets):
        k_id = ids(iota((1, size), 1), offset)
        bias[:, n * size : (n + 1) * size] = jnp.where(q_id == k_id, 0.0, NEG)
    scale = (feats // HC) ** -0.5
    for pair in range(feats // 128):
        lanes = pl.ds(pair * 128, 128)
        mix[:, lanes] = head_pair(
            queries[:, pair * 128 : (pair + 1) * 128],
            (keys[:, lanes],),
            (values[:, lanes],),
            None,
            bias[...],
            scale,
        ).astype(BF16)
    out = own_ref[...].astype(F32).reshape(size, feats) + dot(mix[...], proj_ref[...])
    out_ref[...] = out.astype(BF16).reshape(out_ref.shape)


def expand_kernel(
    shift_ref, own_ref, other_ref, fkeep_ref, fother_ref, gain_ref, weight_ref,
    out_ref, cs, ex, *, own_cols,
):
    core = lax.axis_index("lon") % 2
    slots, depth, feats = own_ref.shape
    size = slots * depth
    units = size // own_cols
    rows = 2 * units // slots
    home = own_cols // 2
    a1, a2 = shift_ref[0, 0], shift_ref[1, 0]
    put(cs.at[0], 0, own_ref[...].astype(F32).reshape(size, feats))
    put(cs.at[1], 0, other_ref[...].astype(F32).reshape(size, feats))
    blocks = []
    for which in range(2):
        for col in range(home):
            blocks.append(take(cs.at[which], core * home + col, units, own_cols))
    blocks = jnp.concatenate(blocks, axis=0).astype(BF16)
    gain = gain_ref[...]
    for q in range(2):
        for p in range(2):
            k = 2 * q + p
            piece = layer_norm(dot(blocks, weight_ref[:, k * feats : (k + 1) * feats]), gain)
            for which in range(2):
                for col in range(home):
                    first = (which * home + col) * units
                    put(ex.at[which, 2 * col + q], p, piece[first : first + units], 2)
    for which, (target, f_ref) in enumerate(((core, fkeep_ref), (1 - core, fother_ref))):
        for slot in range(slots):
            level = level_of(target, slot, a1)
            source = which if slot == 0 else jnp.where(a1 == a2, which, 1 - which)
            for col in range(2 * home):
                add = take(ex.at[source, col], slot * rows, rows)
                out_ref[level, col] = (f_ref[col, slot].astype(F32) + add).astype(BF16)


VMEM_SPEC = pl.BlockSpec(memory_space=pltpu.VMEM)
SMEM_SPEC = pl.BlockSpec(memory_space=pltpu.SMEM)


def call(kernel, name, outs, scratch, arrays, limit):
    return pl.pallas_call(
        kernel,
        name=name,
        out_shape=outs,
        in_specs=[SMEM_SPEC] + [VMEM_SPEC] * (len(arrays) - 1),
        out_specs=jax.tree.map(lambda _: VMEM_SPEC, outs),
        scratch_shapes=scratch,
        compiler_params=pltpu.CompilerParams(vmem_limit_bytes=limit << 20),
    )(*arrays)


def local(
    tokens,
    window_shift,
    fine_gain,
    fine_qkv,
    fine_proj,
    merge_gain,
    merge_weight,
    coarse_gain,
    coarse_qkv,
    coarse_proj,
    expand_weight,
    expand_gain,
):
    levels, rows, dev_cols, feats = tokens.shape
    cols = 2 * dev_cols
    slots = 2
    assert levels == 4 and cols == WIN_LON and rows % (2 * WIN_LAT) == 0
    core = lax.axis_index("lon") % 2
    sds = jax.ShapeDtypeStruct
    viewed = tokens.transpose(0, 2, 1, 3)

    def picked(target):
        levels_in = [
            lax.dynamic_index_in_dim(viewed, level_of(target, slot, window_shift[0, 0]), 0, False)
            for slot in range(slots)
        ]
        return jnp.stack(levels_in, axis=1)

    other = swapped(picked(1 - core))
    keep = picked(core)
    grid = jnp.concatenate(
        [jnp.where(core == 0, keep, other), jnp.where(core == 0, other, keep)], axis=0
    )

    def branch(c):
        def run(grid):
            if c == 0:
                return grid
            left = permuted(grid[: cols - c], -2)
            right = permuted(grid[cols - c :], 2)
            return jnp.concatenate([left, right], axis=0)

        return run

    around = lax.switch(window_shift[0, 2], [branch(c) for c in range(WIN_LON)], grid)
    unit = slots * cols
    tokens_n = rows * unit
    size = WIN_LAT * unit
    channels = merge_weight.shape[1]
    coarse_depth = rows // 2 * dev_cols
    coarse_n = slots * coarse_depth
    coarse_type = sds((slots, coarse_depth, channels), BF16)
    fine_half = sds((dev_cols, slots, rows, feats), BF16)
    fine_keep, fine_send, coarse = call(
        fine_kernel, "fine", (fine_half, fine_half, coarse_type),
        [
            chunked(tokens_n + size, feats),
            chunked(tokens_n + size, feats),
            pltpu.VMEM((tokens_n, 3 * feats), BF16),
            pltpu.VMEM((tokens_n, 2 * feats), BF16),
            pltpu.VMEM((tokens_n, feats), BF16),
            chunked(tokens_n, feats),
            chunked(tokens_n, feats),
            pltpu.VMEM((2, 2 * size, size), F32),
        ],
        (
            window_shift, grid, around, fine_gain.reshape(1, feats), fine_qkv, fine_proj,
            merge_gain.reshape(1, 4 * feats), merge_weight,
        ),
        FINE_MIB,
    )
    fine_other = swapped(fine_send)
    moved = jnp.where(window_shift[0, 0] != window_shift[1, 0], swapped(coarse[1]), coarse[1])
    coarse = jnp.stack([coarse[0], moved])
    l1, r1 = permuted(coarse, 2), permuted(coarse, -2)
    l2, r2 = permuted(coarse, 4), permuted(coarse, -4)
    coarse_out = call(
        functools.partial(coarse_kernel, own_cols=dev_cols), "coarse", coarse_type,
        [
            pltpu.VMEM((5 * coarse_n, channels), BF16),
            pltpu.VMEM((5 * coarse_n, channels), BF16),
            pltpu.VMEM((2 * coarse_n, 5 * coarse_n), F32),
            pltpu.VMEM((coarse_n, channels), BF16),
        ],
        (
            window_shift, coarse, l1, r1, l2, r2, coarse_gain.reshape(1, channels), coarse_qkv,
            coarse_proj,
        ),
        COARSE_MIB,
    )
    coarse_other = swapped(coarse_out)
    out = call(
        functools.partial(expand_kernel, own_cols=dev_cols), "expand",
        sds(viewed.shape, BF16),
        [
            pltpu.VMEM((2, channels // 128, coarse_n, 128), F32),
            pltpu.VMEM((2, dev_cols, feats // 128, slots * rows, 128), F32),
        ],
        (
            window_shift, coarse_out, coarse_other, fine_keep, fine_other,
            expand_gain.reshape(1, feats), expand_weight,
        ),
        EXPAND_MIB,
    )
    return out.transpose(0, 2, 1, 3)


def solution(mesh):
    placed = (P("groups", None, "lon", None), P(), P(), P(), P(), P(), P(), P(), P(), P(), P(), P())
    return jax.shard_map(
        local, mesh=mesh, in_specs=placed, out_specs=P("groups", None, "lon", None), check_vma=False
    )
```

```python
import functools

import jax
import jax.numpy as jnp
from jax import lax
from jax.experimental import pallas as pl
from jax.experimental.pallas import tpu as pltpu
from jax.sharding import PartitionSpec as P

HEADS = 8
HC = 8
WIN_LEV = 2
WIN_LAT = 6
WIN_LON = 12
EPSILON = 1e-05
NEG = -1e30
OWN_MIB = 8
FINE_MIB = 24
COARSE_MIB = 16
EXPAND_MIB = 16
F32 = jnp.float32
BF16 = jnp.bfloat16


def permuted(value, steps):
    count = lax.axis_size("lon")
    return lax.ppermute(value, "lon", [(s, (s + steps) % count) for s in range(count)])


def swapped(value):
    count = lax.axis_size("lon")
    return lax.ppermute(value, "lon", [(s, s ^ 1) for s in range(count)])


def layer_norm(x, gain):
    center = x - jnp.mean(x, axis=-1, keepdims=True)
    spread = jnp.mean(center * center, axis=-1, keepdims=True)
    return center * lax.rsqrt(spread + EPSILON) * gain


def dot(a, b):
    return jnp.dot(a, b, preferred_element_type=F32)


def dot_t(a, b):
    return lax.dot_general(a, b, (((1,), (1,)), ((), ())), preferred_element_type=F32)


def level_of(core, slot, a):
    if slot == 0:
        return 2 * core
    return jnp.where(core == 0, 1 + 2 * a, 3 - 2 * a)


def iota(shape, axis):
    return lax.broadcasted_iota(jnp.int32, shape, axis)


def take(ref, start, count, stride=1):
    at = pl.ds(start, count, stride=stride) if stride > 1 else pl.ds(start, count)
    return jnp.concatenate([ref[k, at, :] for k in range(ref.shape[0])], axis=1)


def put(ref, start, value, stride=1):
    at = pl.ds(start, value.shape[0], stride=stride) if stride > 1 else pl.ds(start, value.shape[0])
    for k in range(ref.shape[0]):
        ref[k, at, :] = value[:, k * 128 : (k + 1) * 128]


def chunked(count, width):
    return pltpu.VMEM((width // 128, count, 128), F32)


def head_pair(q, keys, values, picks, bias, scale):
    size = q.shape[0]
    low = iota(q.shape, 1) < q.shape[1] // 2
    zero = jnp.zeros_like(q)
    q2 = jnp.concatenate([jnp.where(low, q, zero), jnp.where(low, zero, q)], axis=0)
    if picks is None:
        scores = dot_t(q2, keys[0])
    else:
        scores = jnp.where(picks, dot_t(q2, keys[0]), dot_t(q2, keys[1]))
    scores = scores + bias
    top = jnp.max(scores, axis=-1, keepdims=True)
    expo = jnp.exp((scores - top) * scale)
    total = jnp.sum(expo, axis=-1, keepdims=True)
    if picks is None:
        mixed = dot(expo.astype(BF16), values[0])
    else:
        none = jnp.zeros_like(expo)
        mixed = dot(jnp.where(picks, expo, none).astype(BF16), values[0]) + dot(
            jnp.where(picks, none, expo).astype(BF16), values[1]
        )
    mixed = mixed / total
    return jnp.where(low, mixed[:size], mixed[size:])


def split_kernel(shift_ref, tok_ref, keep_ref, send_ref, branch_ref, sems):
    core = lax.axis_index("lon") % 2
    a = shift_ref[0, 0]
    copies = []
    for n, (target, out_ref) in enumerate(((1 - core, send_ref), (core, keep_ref))):
        for slot in range(2):
            copies.append(
                pltpu.make_async_copy(
                    tok_ref.at[level_of(target, slot, a)], out_ref.at[:, slot], sems.at[n, slot]
                )
            )
    for copy in copies:
        copy.start()
    branch_ref[0] = shift_ref[0, 2]
    branch_ref[1] = jnp.where(a == shift_ref[1, 0], 0, 1)
    for copy in copies:
        copy.wait()


def by_window(columns, scr):
    cols, slots = len(columns), 2
    unit = slots * cols
    size = WIN_LAT * unit
    for col, read in enumerate(columns):
        for slot in range(slots):
            put(scr, size + slot * cols + col, read(slot), unit)
    put(scr, 0, take(scr, scr.shape[1] - size, size))


def reader(ref, col):
    return lambda slot: ref[col, slot].astype(F32)


def own_kernel(shift_ref, x_ref, gain_ref, qkv_ref, xw_ref, out_ref, xs):
    cols, slots, rows, feats = x_ref.shape
    unit = slots * cols
    size = WIN_LAT * unit
    b = shift_ref[0, 1]
    by_window([reader(x_ref, col) for col in range(cols)], xs)
    gain = gain_ref[...]

    @pl.loop(0, rows // WIN_LAT)
    def _(j):
        at = pl.ds(pl.multiple_of(j * size, size), size)
        tokens = take(xs, pl.multiple_of(((j + 1) * WIN_LAT - b) * unit, 8), size)
        xw_ref[at, :] = tokens.astype(BF16)
        normed = layer_norm(tokens, gain).astype(BF16)
        out_ref[at, :] = dot(normed, qkv_ref[...]).astype(BF16)


def fine_kernel(
    shift_ref, r_ref, xw_ref, qkv, gain_ref, qkv_hbm, proj_hbm, mgain_ref, mw_hbm,
    keep_ref, send_ref, coarse_ref,
    rs, kvr, mix, fr, fu, bias, kv_w, proj_ref, mw_ref, sems,
):
    core = lax.axis_index("lon") % 2
    cols, slots, rows, feats = r_ref.shape
    own_cols = cols // 2
    unit = slots * cols
    wins = rows // WIN_LAT
    size = WIN_LAT * unit
    a, b, c = shift_ref[0, 0], shift_ref[0, 1], shift_ref[0, 2]
    loads = [
        pltpu.make_async_copy(source, target, sems.at[n])
        for n, (source, target) in enumerate(
            (
                (qkv_hbm.at[:, pl.ds(feats, 2 * feats)], kv_w),
                (proj_hbm, proj_ref),
                (mw_hbm, mw_ref),
            )
        )
    ]
    for load in loads:
        load.start()
    by_window([reader(r_ref, col) for col in range(cols)], rs)
    gain = gain_ref[...]
    loads[0].wait()
    for j in range(wins):
        tokens = take(rs, pl.multiple_of(((j + 1) * WIN_LAT - b) * unit, 8), size)
        normed = layer_norm(tokens, gain).astype(BF16)
        kvr[pl.ds(j * size, size), :] = dot(normed, kv_w[...]).astype(BF16)
    def parts(index):
        return index // unit, (index // cols) % slots, index % cols

    q_row, q_slot, q_col = parts(iota((2 * size, 1), 0) % size)
    k_row, k_slot, k_col = parts(iota((1, size), 1))
    q_side = jnp.where(q_col + c >= cols, 1, 0)
    k_side = jnp.where(k_col + c >= cols, 1, 0)
    apart = jnp.where((a == 0) | (core == 1), 0, 1)
    q_slot, k_slot = q_slot * apart, k_slot * apart
    q_id = q_slot * 2 + jnp.where(q_row < b, 1, 0)
    k_id = k_slot * 2 + jnp.where(k_row < b, 1, 0)
    bias[0] = jnp.where(q_id == k_id, 0.0, NEG)
    bias[1] = jnp.where(q_slot == k_slot, 0.0, NEG)
    scale = (feats // HEADS) ** -0.5

    for j in range(wins):
        at = pl.ds(j * size, size)
        masked = bias[min(j, 1)]
        picks = q_side == k_side
        for pair in range(feats // 128):
            lanes = pl.ds(pair * 128, 128)
            k_lanes = pl.ds(feats + pair * 128, 128)
            v_lanes = pl.ds(2 * feats + pair * 128, 128)
            mix[at, lanes] = head_pair(
                qkv[at, lanes],
                (qkv[at, k_lanes], kvr[at, lanes]),
                (qkv[at, v_lanes], kvr[at, k_lanes]),
                picks,
                masked,
                scale,
            ).astype(BF16)

    half = rows // 2
    loads[1].wait()
    for j in range(wins):
        at = pl.ds(j * size, size)
        fine = xw_ref[at, :].astype(F32) + dot(mix[at, :], proj_ref[...])
        fine = fine.astype(BF16).astype(F32)
        for inner in range(WIN_LAT):
            source = j * WIN_LAT + inner - b
            source = jnp.where(source < 0, source + rows, source)
            put(fr, pl.multiple_of(source * unit, 8), fine[inner * unit : (inner + 1) * unit])

    for p in range(2):
        for slot in range(slots):
            for col in range(cols):
                first = slot * cols + col
                piece = take(fr, p * unit + first, half, 2 * unit)
                put(fu, (p * slots + slot) * half * cols + col, piece, cols)
    loads[2].wait()
    groups = []
    count = half * unit // 2
    for q in range(2):
        for p in range(2):
            groups.append(take(fu, p * half * unit + q, count, 2))
    width = 4 * feats
    mean = sum(jnp.sum(piece, axis=-1, keepdims=True) for piece in groups) / width
    groups = [piece - mean for piece in groups]
    spread = sum(jnp.sum(piece * piece, axis=-1, keepdims=True) for piece in groups) / width
    scaling = lax.rsqrt(spread + EPSILON)
    total = jnp.zeros((count, mw_ref.shape[1]), F32)
    for k, piece in enumerate(groups):
        lanes = slice(k * feats, (k + 1) * feats)
        merged = (piece * scaling * mgain_ref[:, lanes]).astype(BF16)
        total = total + dot(merged, mw_ref[lanes, :])
    coarse_ref[...] = total.astype(BF16).reshape(coarse_ref.shape)
    for slot in range(slots):
        for col in range(own_cols):
            for target, out_ref in ((core, keep_ref), (1 - core, send_ref)):
                start = slot * cols + target * own_cols + col
                out_ref[col, slot] = take(fr, start, rows, unit).astype(BF16)


def coarse_kernel(
    shift_ref, own_ref, l1_ref, r1_ref, l2_ref, r2_ref, gain_ref, qkv_ref, proj_ref,
    out_ref, keys, values, bias, mix, *, own_cols,
):
    place = lax.axis_index("lon")
    core = place % 2
    chips_wide = WIN_LON // own_cols
    side = (place // 2) % chips_wide
    slots, depth, feats = own_ref.shape
    size = slots * depth
    a, b, c = shift_ref[1, 0], shift_ref[1, 1], shift_ref[1, 2]
    gain = gain_ref[...]
    refs = (own_ref, l1_ref, r1_ref, l2_ref, r2_ref)
    offsets = (0, -1, 1, -2, 2)
    queries = None
    for n, ref in enumerate(refs):
        at = pl.ds(n * size, size)
        full = ref[...].astype(F32).reshape(size, feats)
        normed = layer_norm(full, gain).astype(BF16)
        if n == 0:
            queries = dot(normed, qkv_ref[:, :feats]).astype(BF16)
        keys[at, :] = dot(normed, qkv_ref[:, feats : 2 * feats]).astype(BF16)
        values[at, :] = dot(normed, qkv_ref[:, 2 * feats :]).astype(BF16)

    def ids(index, offset):
        slot = index // depth
        row = (index // own_cols) % (depth // own_cols)
        col = (side + offset + chips_wide) * own_cols + index % own_cols
        window = (col + c) // WIN_LON
        apart = jnp.where((a == 0) | (core == 1), 0, slot)
        return (window * 8 + (row + b) // WIN_LAT) * 2 + apart

    q_id = ids(iota((2 * size, 1), 0) % size, 0)
    for n, offset in enumerate(offsets):
        k_id = ids(iota((1, size), 1), offset)
        bias[:, n * size : (n + 1) * size] = jnp.where(q_id == k_id, 0.0, NEG)
    scale = (feats // HC) ** -0.5
    for pair in range(feats // 128):
        lanes = pl.ds(pair * 128, 128)
        mix[:, lanes] = head_pair(
            queries[:, pair * 128 : (pair + 1) * 128],
            (keys[:, lanes],),
            (values[:, lanes],),
            None,
            bias[...],
            scale,
        ).astype(BF16)
    out = own_ref[...].astype(F32).reshape(size, feats) + dot(mix[...], proj_ref[...])
    out_ref[...] = out.astype(BF16).reshape(out_ref.shape)


def expand_kernel(
    shift_ref, own_ref, other_ref, fkeep_ref, fother_ref, gain_ref, weight_ref,
    out_ref, cs, ex, *, own_cols,
):
    core = lax.axis_index("lon") % 2
    slots, depth, feats = own_ref.shape
    size = slots * depth
    units = size // own_cols
    rows = 2 * units // slots
    home = own_cols // 2
    a1, a2 = shift_ref[0, 0], shift_ref[1, 0]
    put(cs.at[0], 0, own_ref[...].astype(F32).reshape(size, feats))
    put(cs.at[1], 0, other_ref[...].astype(F32).reshape(size, feats))
    blocks = []
    for which in range(2):
        for col in range(home):
            blocks.append(take(cs.at[which], core * home + col, units, own_cols))
    blocks = jnp.concatenate(blocks, axis=0).astype(BF16)
    gain = gain_ref[...]
    for q in range(2):
        for p in range(2):
            k = 2 * q + p
            piece = layer_norm(dot(blocks, weight_ref[:, k * feats : (k + 1) * feats]), gain)
            for which in range(2):
                for col in range(home):
                    first = (which * home + col) * units
                    put(ex.at[which, 2 * col + q], p, piece[first : first + units], 2)
    for which, (target, f_ref) in enumerate(((core, fkeep_ref), (1 - core, fother_ref))):
        for slot in range(slots):
            level = level_of(target, slot, a1)
            source = which if slot == 0 else jnp.where(a1 == a2, which, 1 - which)
            for col in range(2 * home):
                add = take(ex.at[source, col], slot * rows, rows)
                out_ref[level, col] = (f_ref[col, slot].astype(F32) + add).astype(BF16)


VMEM_SPEC = pl.BlockSpec(memory_space=pltpu.VMEM)
SMEM_SPEC = pl.BlockSpec(memory_space=pltpu.SMEM)


HBM_SPEC = pl.BlockSpec(memory_space=pltpu.HBM)


def call(kernel, name, outs, scratch, arrays, limit, cost=None, hbm=()):
    specs = [SMEM_SPEC] + [VMEM_SPEC] * (len(arrays) - 1)
    arrays = list(arrays)
    for n in hbm:
        specs[n] = HBM_SPEC
        arrays[n] = pltpu.with_memory_space_constraint(arrays[n], pltpu.HBM)
    return pl.pallas_call(
        kernel,
        name=name,
        out_shape=outs,
        in_specs=specs,
        out_specs=jax.tree.map(lambda _: VMEM_SPEC, outs),
        scratch_shapes=scratch,
        compiler_params=pltpu.CompilerParams(vmem_limit_bytes=limit << 20),
        cost_estimate=cost,
    )(*arrays)


def local(
    tokens,
    window_shift,
    fine_gain,
    fine_qkv,
    fine_proj,
    merge_gain,
    merge_weight,
    coarse_gain,
    coarse_qkv,
    coarse_proj,
    expand_weight,
    expand_gain,
):
    levels, rows, dev_cols, feats = tokens.shape
    cols = 2 * dev_cols
    slots = 2
    assert levels == 4 and cols == WIN_LON and rows % (2 * WIN_LAT) == 0
    core = lax.axis_index("lon") % 2
    sds = jax.ShapeDtypeStruct
    viewed = tokens.transpose(0, 2, 1, 3)

    half = sds((dev_cols, slots, rows, feats), BF16)
    vhalf = pltpu.VMEM(half.shape, BF16)
    keep, send, index = pl.pallas_call(
        split_kernel,
        name="split",
        out_shape=(vhalf, vhalf, sds((2,), jnp.int32)),
        in_specs=[SMEM_SPEC, HBM_SPEC],
        out_specs=(VMEM_SPEC, VMEM_SPEC, SMEM_SPEC),
        scratch_shapes=[pltpu.SemaphoreType.DMA((2, slots))],
        compiler_params=pltpu.CompilerParams(vmem_limit_bytes=4 << 20),
    )(window_shift, pltpu.with_memory_space_constraint(viewed, pltpu.HBM))
    other = swapped(send)
    grid = jnp.concatenate(
        [jnp.where(core == 0, keep, other), jnp.where(core == 0, other, keep)], axis=0
    )
    unit = slots * cols
    tokens_n = rows * unit
    size = WIN_LAT * unit
    gain = fine_gain.reshape(1, feats)

    channels = merge_weight.shape[1]
    coarse_depth = rows // 2 * dev_cols
    coarse_n = slots * coarse_depth
    coarse_type = sds((slots, coarse_depth, channels), BF16)

    def branch(c):
        def run(grid):
            around = grid
            if c > 0:
                left = permuted(grid[: cols - c], -2)
                right = permuted(grid[cols - c :], 2)
                around = jnp.concatenate([left, right], axis=0)
            own = call(
                own_kernel, "own",
                (pltpu.VMEM((tokens_n, feats), BF16), pltpu.VMEM((tokens_n, 3 * feats), BF16)),
                [chunked(tokens_n + size, feats)],
                (window_shift, grid, gain, fine_qkv),
                OWN_MIB,
                pl.CostEstimate(
                    flops=tokens_n * feats * feats * 6,
                    bytes_accessed=10 * tokens_n * feats,
                    transcendentals=0,
                ),
            )
            return around, *own

        return run

    branches = [branch(c) for c in range(WIN_LON)]
    around, xw, qkv = lax.switch(index[0], branches, grid)
    fine_keep, fine_send, coarse = call(
        fine_kernel, "fine", (half, half, coarse_type),
        [
            chunked(tokens_n + size, feats),
            pltpu.VMEM((tokens_n, 2 * feats), BF16),
            pltpu.VMEM((tokens_n, feats), BF16),
            chunked(tokens_n, feats),
            chunked(tokens_n, feats),
            pltpu.VMEM((2, 2 * size, size), F32),
            pltpu.VMEM((feats, 2 * feats), BF16),
            pltpu.VMEM(fine_proj.shape, BF16),
            pltpu.VMEM(merge_weight.shape, BF16),
            pltpu.SemaphoreType.DMA((3,)),
        ],
        (
            window_shift, around, xw, qkv, gain, fine_qkv, fine_proj,
            merge_gain.reshape(1, 4 * feats), merge_weight,
        ),
        FINE_MIB,
        hbm=(5, 6, 8),
    )
    fine_other = swapped(fine_send)
    moved = jnp.where(index[1] == 1, swapped(coarse[1]), coarse[1])
    coarse = jnp.stack([coarse[0], moved])
    l1, r1 = permuted(coarse, 2), permuted(coarse, -2)
    l2, r2 = permuted(coarse, 4), permuted(coarse, -4)
    coarse_out = call(
        functools.partial(coarse_kernel, own_cols=dev_cols), "coarse", coarse_type,
        [
            pltpu.VMEM((5 * coarse_n, channels), BF16),
            pltpu.VMEM((5 * coarse_n, channels), BF16),
            pltpu.VMEM((2 * coarse_n, 5 * coarse_n), F32),
            pltpu.VMEM((coarse_n, channels), BF16),
        ],
        (
            window_shift, coarse, l1, r1, l2, r2, coarse_gain.reshape(1, channels), coarse_qkv,
            coarse_proj,
        ),
        COARSE_MIB,
    )
    coarse_other = swapped(coarse_out)
    out = call(
        functools.partial(expand_kernel, own_cols=dev_cols), "expand",
        sds(viewed.shape, BF16),
        [
            pltpu.VMEM((2, channels // 128, coarse_n, 128), F32),
            pltpu.VMEM((2, dev_cols, feats // 128, slots * rows, 128), F32),
        ],
        (
            window_shift, coarse_out, coarse_other, fine_keep, fine_other,
            expand_gain.reshape(1, feats), expand_weight,
        ),
        EXPAND_MIB,
    )
    return out.transpose(0, 2, 1, 3)


def solution(mesh):
    placed = (P("groups", None, "lon", None), P(), P(), P(), P(), P(), P(), P(), P(), P(), P(), P())
    return jax.shard_map(
        local, mesh=mesh, in_specs=placed, out_specs=P("groups", None, "lon", None), check_vma=False
    )
```

```python
import jax
import jax.numpy as jnp
from jax import lax
from jax.experimental import pallas as pl
from jax.experimental.pallas import tpu as pltpu
from jax.sharding import PartitionSpec as P


HEADS = 8
HC = 8
WIN_LAT = 6
WIN_LON = 12
EPSILON = 1e-05
NEG = -1e30
OWN_MIB = 8
FINE_MIB = 24
COARSE_MIB = 16
EXPAND_MIB = 16
F32 = jnp.float32
BF16 = jnp.bfloat16


def permuted(value, steps):
    count = lax.axis_size("lon")
    return lax.ppermute(value, "lon", [(s, (s + steps) % count) for s in range(count)])


def swapped(value):
    count = lax.axis_size("lon")
    return lax.ppermute(value, "lon", [(s, s ^ 1) for s in range(count)])


def paired(value, inside):
    count = lax.axis_size("lon")
    steps = [2 if (s // 2 % 2 == 0) == inside else -2 for s in range(count)]
    return lax.ppermute(value, "lon", [(s, (s + steps[s]) % count) for s in range(count)])


def layer_norm(x, gain):
    center = x - jnp.mean(x, axis=-1, keepdims=True)
    spread = jnp.mean(center * center, axis=-1, keepdims=True)
    return center * lax.rsqrt(spread + EPSILON) * gain


def dot(a, b):
    return jnp.dot(a, b, preferred_element_type=F32)


def dot_t(a, b):
    return lax.dot_general(a, b, (((1,), (1,)), ((), ())), preferred_element_type=F32)


def level_of(core, slot, a):
    if slot == 0:
        return 2 * core
    return jnp.where(core == 0, 1 + 2 * a, 3 - 2 * a)


def iota(shape, axis):
    return lax.broadcasted_iota(jnp.int32, shape, axis)


def take(ref, start, count, stride=1):
    at = pl.ds(start, count, stride=stride) if stride > 1 else pl.ds(start, count)
    return jnp.concatenate([ref[k, at, :] for k in range(ref.shape[0])], axis=1)


def put(ref, start, value, stride=1):
    at = pl.ds(start, value.shape[0], stride=stride) if stride > 1 else pl.ds(start, value.shape[0])
    for k in range(ref.shape[0]):
        ref[k, at, :] = value[:, k * 128 : (k + 1) * 128]


def chunked(count, width):
    return pltpu.VMEM((width // 128, count, 128), F32)


def head_pair(q, k, v, bias, scale, far=None):
    size = q.shape[0]
    low = iota(q.shape, 1) < 64
    zero = jnp.zeros_like(q)
    q2 = [jnp.where(low, q, zero), jnp.where(low, zero, q)]
    if far is not None:
        q2 = [
            jnp.concatenate([jnp.where(far, zero, one), jnp.where(far, one, zero)], axis=1)
            for one in q2
        ]
    scores = dot_t(jnp.concatenate(q2, axis=0), k) + bias
    top = jnp.max(scores, axis=-1, keepdims=True)
    expo = jnp.exp((scores - top) * scale)
    total = jnp.sum(expo, axis=-1, keepdims=True)
    mixed = dot(expo.astype(BF16), v) / total
    if far is not None:
        mixed = [
            jnp.where(far, part[:, 128:], part[:, :128]) for part in (mixed[:size], mixed[size:])
        ]
    else:
        mixed = [mixed[:size], mixed[size:]]
    return jnp.where(low, mixed[0], mixed[1])


def both_ways(far, one, two):
    return jnp.concatenate([jnp.where(far, two, one), jnp.where(far, one, two)], axis=1)


def split_kernel(shift_ref, tok_ref, keep_ref, send_ref, branch_ref):
    core = lax.axis_index("lon") % 2
    a = shift_ref[0, 0]
    branch_ref[0] = shift_ref[0, 2]
    branch_ref[1] = jnp.where(a == shift_ref[1, 0], 0, 1)
    for target, out_ref in ((1 - core, send_ref), (core, keep_ref)):
        for slot in range(2):
            level = level_of(target, slot, a)
            for col in range(out_ref.shape[0]):
                out_ref[col, slot] = tok_ref[level, col]


def by_window(columns, scr):
    cols, slots = len(columns), 2
    unit = slots * cols
    size = WIN_LAT * unit
    for col, read in enumerate(columns):
        for slot in range(slots):
            put(scr, size + slot * cols + col, read(slot), unit)
    put(scr, 0, take(scr, scr.shape[1] - size, size))


def reader(ref, col):
    return lambda slot: ref[col, slot].astype(F32)


def own_kernel(shift_ref, x_ref, gain_ref, qkv_ref, xw_ref, out_ref, xs):
    cols, slots, rows, _ = x_ref.shape
    unit = slots * cols
    size = WIN_LAT * unit
    b = shift_ref[0, 1]
    by_window([reader(x_ref, col) for col in range(cols)], xs)
    gain = gain_ref[...]

    @pl.loop(0, rows // WIN_LAT)
    def _(j):
        at = pl.ds(pl.multiple_of(j * size, size), size)
        tokens = take(xs, pl.multiple_of(((j + 1) * WIN_LAT - b) * unit, 8), size)
        xw_ref[at, :] = tokens.astype(BF16)
        normed = layer_norm(tokens, gain).astype(BF16)
        out_ref[at, :] = dot(normed, qkv_ref[...]).astype(BF16)


def fine_kernel(
    shift_ref, r_ref, xw_ref, qkv, gain_ref, qkv_hbm, proj_hbm, mgain_ref, mw_hbm,
    keep_ref, send_ref, coarse_ref,
    rs, kvr, mix, fr, fu, bias, kv_w, proj_ref, mw_ref, sems,
):
    core = lax.axis_index("lon") % 2
    cols, slots, rows, feats = r_ref.shape
    own_cols = cols // 2
    unit = slots * cols
    wins = rows // WIN_LAT
    size = WIN_LAT * unit
    a, b, c = shift_ref[0, 0], shift_ref[0, 1], shift_ref[0, 2]
    loads = [
        pltpu.make_async_copy(source, target, sems.at[n])
        for n, (source, target) in enumerate(
            (
                (qkv_hbm.at[:, pl.ds(feats, 2 * feats)], kv_w),
                (proj_hbm, proj_ref),
                (mw_hbm, mw_ref),
            )
        )
    ]
    for load in loads:
        load.start()
    by_window([reader(r_ref, col) for col in range(cols)], rs)
    gain = gain_ref[...]
    loads[0].wait()
    for j in range(wins):
        tokens = take(rs, pl.multiple_of(((j + 1) * WIN_LAT - b) * unit, 8), size)
        normed = layer_norm(tokens, gain).astype(BF16)
        kvr[pl.ds(j * size, size), :] = dot(normed, kv_w[...]).astype(BF16)

    def parts(index):
        return index // unit, (index // cols) % slots, index % cols

    q_row, q_slot, _ = parts(iota((2 * size, 1), 0) % size)
    k_row, k_slot, _ = parts(iota((1, size), 1))
    far = iota((size, 128), 0) % cols + c >= cols
    apart = jnp.where((a == 0) | (core == 1), 0, 1)
    q_slot, k_slot = q_slot * apart, k_slot * apart
    q_id = q_slot * 2 + jnp.where(q_row < b, 1, 0)
    k_id = k_slot * 2 + jnp.where(k_row < b, 1, 0)
    bias[0] = jnp.where(q_id == k_id, 0.0, NEG)
    bias[1] = jnp.where(q_slot == k_slot, 0.0, NEG)
    scale = (feats // HEADS) ** -0.5

    for j in range(wins):
        at = pl.ds(j * size, size)
        masked = bias[min(j, 1)]
        for pair in range(feats // 128):
            lanes = pl.ds(pair * 128, 128)
            k_lanes = pl.ds(feats + pair * 128, 128)
            v_lanes = pl.ds(2 * feats + pair * 128, 128)
            mix[at, lanes] = head_pair(
                qkv[at, lanes],
                both_ways(far, qkv[at, k_lanes], kvr[at, lanes]),
                both_ways(far, qkv[at, v_lanes], kvr[at, k_lanes]),
                masked,
                scale,
                far,
            ).astype(BF16)

    half = rows // 2
    loads[1].wait()
    for j in range(wins):
        at = pl.ds(j * size, size)
        fine = xw_ref[at, :].astype(F32) + dot(mix[at, :], proj_ref[...])
        fine = fine.astype(BF16).astype(F32)
        for inner in range(WIN_LAT):
            source = j * WIN_LAT + inner - b
            source = jnp.where(source < 0, source + rows, source)
            put(fr, pl.multiple_of(source * unit, 8), fine[inner * unit : (inner + 1) * unit])

    block = slots * half
    for p in range(2):
        for slot in range(slots):
            for col in range(cols):
                piece = take(fr, p * unit + slot * cols + col, half, 2 * unit)
                put(fu, (p * cols + col) * block + slot * half, piece)
    loads[2].wait()
    groups = []
    count = half * unit // 2
    for q in range(2):
        for p in range(2):
            starts = [(p * cols + col) * block for col in range(q, cols, 2)]
            groups.append(jnp.concatenate([take(fu, start, block) for start in starts], axis=0))
    width = 4 * feats
    mean = sum(jnp.sum(piece, axis=-1, keepdims=True) for piece in groups) / width
    groups = [piece - mean for piece in groups]
    spread = sum(jnp.sum(piece * piece, axis=-1, keepdims=True) for piece in groups) / width
    scaling = lax.rsqrt(spread + EPSILON)
    total = jnp.zeros((count, mw_ref.shape[1]), F32)
    for k, piece in enumerate(groups):
        lanes = slice(k * feats, (k + 1) * feats)
        merged = (piece * scaling * mgain_ref[:, lanes]).astype(BF16)
        total = total + dot(merged, mw_ref[lanes, :])
    coarse_ref[...] = total.astype(BF16).reshape(coarse_ref.shape)
    for slot in range(slots):
        for col in range(own_cols):
            for target, out_ref in ((core, keep_ref), (1 - core, send_ref)):
                start = slot * cols + target * own_cols + col
                out_ref[col, slot] = take(fr, start, rows, unit).astype(BF16)


def coarse_kernel(
    shift_ref, own_ref, inside_ref, outside_ref, left_ref, right_ref, gain_ref, qkv_ref, proj_ref,
    out_ref, keys, values, bias, mix,
):
    place = lax.axis_index("lon")
    core = place % 2
    own_cols, depth, feats = own_ref.shape
    side = (place // 2) % (WIN_LON // own_cols)
    size = own_cols * depth
    a, b, c = shift_ref[1, 0], shift_ref[1, 1], shift_ref[1, 2]
    gain = gain_ref[...]
    near_cols = own_cols - lax.rem(c, own_cols)
    far = [
        jnp.where(col < near_cols, right_ref[col].astype(F32), left_ref[col].astype(F32))
        for col in range(own_cols)
    ]
    queries = None
    sets = [ref[...].astype(F32).reshape(size, feats) for ref in (own_ref, inside_ref, outside_ref)]
    for n, full in enumerate((*sets, jnp.concatenate(far, axis=0))):
        at = pl.ds(n * size, size)
        normed = layer_norm(full, gain).astype(BF16)
        if n == 0:
            queries = dot(normed, qkv_ref[:, :feats]).astype(BF16)
        keys[at, :] = dot(normed, qkv_ref[:, feats : 2 * feats]).astype(BF16)
        values[at, :] = dot(normed, qkv_ref[:, 2 * feats :]).astype(BF16)

    def ids(index, chips):
        col = index // depth
        slot = (index // (depth // 2)) % 2
        row = index % (depth // 2)
        window = ((side + chips(col) + 2) * own_cols + col + c) // WIN_LON
        apart = jnp.where((a == 0) | (core == 1), 0, slot)
        return (window * 8 + (row + b) // WIN_LAT) * 2 + apart

    chips_off = (
        lambda col: 0,
        lambda col: 1 - 2 * side,
        lambda col: 2 * side - 1,
        lambda col: jnp.where(col < near_cols, 2, -2),
    )
    q_id = ids(iota((2 * size, 1), 0) % size, chips_off[0])
    for n, chips in enumerate(chips_off):
        k_id = ids(iota((1, size), 1), chips)
        bias[:, n * size : (n + 1) * size] = jnp.where(q_id == k_id, 0.0, NEG)
    scale = (feats // HC) ** -0.5
    for pair in range(feats // 128):
        lanes = pl.ds(pair * 128, 128)
        mix[:, lanes] = head_pair(
            queries[:, pair * 128 : (pair + 1) * 128],
            keys[:, lanes],
            values[:, lanes],
            bias[...],
            scale,
        ).astype(BF16)
    out = own_ref[...].astype(F32).reshape(size, feats) + dot(mix[...], proj_ref[...])
    out_ref[...] = out.astype(BF16).reshape(out_ref.shape)


def expand_kernel(
    shift_ref, own_ref, other_ref, fkeep_ref, fother_ref, gain_ref, weight_ref,
    out_ref, ex,
):
    core = lax.axis_index("lon") % 2
    own_cols, units, feats = own_ref.shape
    slots = 2
    rows = 2 * units // slots
    home = own_cols // 2
    a1, a2 = shift_ref[0, 0], shift_ref[1, 0]
    blocks = []
    for ref in (own_ref, other_ref):
        for col in range(home):
            blocks.append(ref[core * home + col].astype(F32))
    blocks = jnp.concatenate(blocks, axis=0).astype(BF16)
    gain = gain_ref[...]
    for q in range(2):
        for p in range(2):
            k = 2 * q + p
            piece = layer_norm(dot(blocks, weight_ref[:, k * feats : (k + 1) * feats]), gain)
            for which in range(2):
                for col in range(home):
                    first = (which * home + col) * units
                    put(ex.at[which, 2 * col + q], p, piece[first : first + units], 2)
    for which, (target, f_ref) in enumerate(((core, fkeep_ref), (1 - core, fother_ref))):
        for slot in range(slots):
            level = level_of(target, slot, a1)
            source = which if slot == 0 else jnp.where(a1 == a2, which, 1 - which)
            for col in range(2 * home):
                add = take(ex.at[source, col], slot * rows, rows)
                out_ref[level, col] = (f_ref[col, slot].astype(F32) + add).astype(BF16)


VMEM_SPEC = pl.BlockSpec(memory_space=pltpu.VMEM)
SMEM_SPEC = pl.BlockSpec(memory_space=pltpu.SMEM)


HBM_SPEC = pl.BlockSpec(memory_space=pltpu.HBM)


def call(kernel, outs, scratch, arrays, limit, cost=None, hbm=()):
    specs = [SMEM_SPEC] + [VMEM_SPEC] * (len(arrays) - 1)
    arrays = list(arrays)
    for n in hbm:
        specs[n] = HBM_SPEC
        arrays[n] = pltpu.with_memory_space_constraint(arrays[n], pltpu.HBM)
    return pl.pallas_call(
        kernel,
        out_shape=outs,
        in_specs=specs,
        out_specs=jax.tree.map(lambda _: VMEM_SPEC, outs),
        scratch_shapes=scratch,
        compiler_params=pltpu.CompilerParams(vmem_limit_bytes=limit << 20),
        cost_estimate=cost,
    )(*arrays)


def local(
    tokens,
    window_shift,
    fine_gain,
    fine_qkv,
    fine_proj,
    merge_gain,
    merge_weight,
    coarse_gain,
    coarse_qkv,
    coarse_proj,
    expand_weight,
    expand_gain,
):
    levels, rows, dev_cols, feats = tokens.shape
    cols = 2 * dev_cols
    slots = 2
    assert levels == 4 and cols == WIN_LON and rows % (2 * WIN_LAT) == 0
    assert lax.axis_size("lon") % 4 == 0 and WIN_LON == 2 * dev_cols
    core = lax.axis_index("lon") % 2
    sds = jax.ShapeDtypeStruct
    viewed = tokens.transpose(0, 2, 1, 3)

    half = sds((dev_cols, slots, rows, feats), BF16)
    vhalf = pltpu.VMEM(half.shape, BF16)
    keep, send, index = pl.pallas_call(
        split_kernel,
        name="split",
        out_shape=(vhalf, vhalf, sds((2,), jnp.int32)),
        in_specs=[SMEM_SPEC, VMEM_SPEC],
        out_specs=(VMEM_SPEC, VMEM_SPEC, SMEM_SPEC),
        compiler_params=pltpu.CompilerParams(vmem_limit_bytes=4 << 20),
    )(window_shift, pltpu.with_memory_space_constraint(viewed, pltpu.HBM))
    other = swapped(send)
    grid = jnp.concatenate(
        [jnp.where(core == 0, keep, other), jnp.where(core == 0, other, keep)], axis=0
    )
    unit = slots * cols
    tokens_n = rows * unit
    size = WIN_LAT * unit
    gain = fine_gain.reshape(1, feats)

    channels = merge_weight.shape[1]
    coarse_depth = rows // 2 * slots
    coarse_n = dev_cols * coarse_depth
    coarse_type = sds((dev_cols, coarse_depth, channels), BF16)

    def branch(c):
        def run(grid):
            around = grid
            if c > 0:
                left = permuted(grid[: cols - c], -2)
                right = permuted(grid[cols - c :], 2)
                around = jnp.concatenate([left, right], axis=0)
            own = call(
                own_kernel,
                (pltpu.VMEM((tokens_n, feats), BF16), pltpu.VMEM((tokens_n, 3 * feats), BF16)),
                [chunked(tokens_n + size, feats)],
                (window_shift, grid, gain, fine_qkv),
                OWN_MIB,
                pl.CostEstimate(
                    flops=tokens_n * feats * feats * 6,
                    bytes_accessed=10 * tokens_n * feats,
                    transcendentals=0,
                ),
            )
            return around, *own

        return run

    branches = [branch(c) for c in range(WIN_LON)]
    around, xw, qkv = lax.switch(index[0], branches, grid)
    fine_keep, fine_send, coarse = call(
        fine_kernel, (half, half, coarse_type),
        [
            chunked(tokens_n + size, feats),
            pltpu.VMEM((tokens_n, 2 * feats), BF16),
            pltpu.VMEM((tokens_n, feats), BF16),
            chunked(tokens_n, feats),
            chunked(tokens_n, feats),
            pltpu.VMEM((2, 2 * size, size), F32),
            pltpu.VMEM((feats, 2 * feats), BF16),
            pltpu.VMEM(fine_proj.shape, BF16),
            pltpu.VMEM(merge_weight.shape, BF16),
            pltpu.SemaphoreType.DMA((3,)),
        ],
        (
            window_shift, around, xw, qkv, gain, fine_qkv, fine_proj,
            merge_gain.reshape(1, 4 * feats), merge_weight,
        ),
        FINE_MIB,
        hbm=(5, 6, 8),
    )
    fine_other = swapped(fine_send)
    upper = jnp.arange(coarse_depth, dtype=jnp.int32)[None, :, None] >= coarse_depth // 2
    coarse = jnp.where(upper & (index[1] == 1), swapped(coarse), coarse)

    right = permuted(coarse, -4)
    outside = paired(coarse, False)
    inside = paired(coarse, True)
    left = permuted(coarse, 4)
    coarse_out = call(
        coarse_kernel, coarse_type,
        [
            pltpu.VMEM((4 * coarse_n, channels), BF16),
            pltpu.VMEM((4 * coarse_n, channels), BF16),
            pltpu.VMEM((2 * coarse_n, 4 * coarse_n), F32),
            pltpu.VMEM((coarse_n, channels), BF16),
        ],
        (
            window_shift, coarse, inside, outside, left, right, coarse_gain.reshape(1, channels), coarse_qkv,
            coarse_proj,
        ),
        COARSE_MIB,
    )
    coarse_other = swapped(coarse_out)
    out = call(
        expand_kernel,
        sds(viewed.shape, BF16),
        [
            pltpu.VMEM((2, dev_cols, feats // 128, slots * rows, 128), F32),
        ],
        (
            window_shift, coarse_out, coarse_other, fine_keep, fine_other,
            expand_gain.reshape(1, feats), expand_weight,
        ),
        EXPAND_MIB,
    )
    return out.transpose(0, 2, 1, 3)


def solution(mesh):
    placed = (P("groups", None, "lon", None), P(), P(), P(), P(), P(), P(), P(), P(), P(), P(), P())
    return jax.shard_map(
        local, mesh=mesh, in_specs=placed, out_specs=P("groups", None, "lon", None), check_vma=False
    )
```

```python
import functools

import jax
import jax.numpy as jnp
from jax import lax
from jax.experimental import pallas as pl
from jax.experimental.pallas import tpu as pltpu
from jax.sharding import PartitionSpec as P


HEADS = 8
HC = 8
WIN_LAT = 6
WIN_LON = 12
EPSILON = 1e-05
NEG = -1e30
FEW = 3
MERGE_MIB = 12
OWN_MIB = 8
FINE_MIB = 24
COARSE_MIB = 16
EXPAND_MIB = 16
F32 = jnp.float32
BF16 = jnp.bfloat16


def permuted(value, steps, flip=0):
    count = lax.axis_size("lon")
    return lax.ppermute(value, "lon", [(s, (s + steps) % count ^ flip) for s in range(count)])


def swapped(value):
    count = lax.axis_size("lon")
    return lax.ppermute(value, "lon", [(s, s ^ 1) for s in range(count)])


def paired(value, inside):
    count = lax.axis_size("lon")
    steps = [2 if (s // 2 % 2 == 0) == inside else -2 for s in range(count)]
    return lax.ppermute(value, "lon", [(s, (s + steps[s]) % count) for s in range(count)])


def layer_norm(x, gain):
    center = x - jnp.mean(x, axis=-1, keepdims=True)
    spread = jnp.mean(center * center, axis=-1, keepdims=True)
    return center * lax.rsqrt(spread + EPSILON) * gain


def dot(a, b):
    return jnp.dot(a, b, preferred_element_type=F32)


def dot_t(a, b):
    return lax.dot_general(a, b, (((1,), (1,)), ((), ())), preferred_element_type=F32)


def level_of(core, slot, a):
    if slot == 0:
        return 2 * core
    return jnp.where(core == 0, 1 + 2 * a, 3 - 2 * a)


def is_wide(c):
    return (c > FEW) & (c < WIN_LON - FEW)


def iota(shape, axis):
    return lax.broadcasted_iota(jnp.int32, shape, axis)


def take(ref, start, count, stride=1):
    at = pl.ds(start, count, stride=stride) if stride > 1 else pl.ds(start, count)
    return jnp.concatenate([ref[k, at, :] for k in range(ref.shape[0])], axis=1)


def put(ref, start, value, stride=1):
    at = pl.ds(start, value.shape[0], stride=stride) if stride > 1 else pl.ds(start, value.shape[0])
    for k in range(ref.shape[0]):
        ref[k, at, :] = value[:, k * 128 : (k + 1) * 128]


def chunked(count, width):
    return pltpu.VMEM((width // 128, count, 128), F32)


def head_pair(q, k, v, bias, scale, far=None):
    size = q.shape[0]
    low = iota(q.shape, 1) < 64
    zero = jnp.zeros_like(q)
    q2 = [jnp.where(low, q, zero), jnp.where(low, zero, q)]
    if far is not None:
        q2 = [
            jnp.concatenate([jnp.where(far, zero, one), jnp.where(far, one, zero)], axis=1)
            for one in q2
        ]
    scores = dot_t(jnp.concatenate(q2, axis=0), k) + bias
    top = jnp.max(scores, axis=-1, keepdims=True)
    expo = jnp.exp((scores - top) * scale)
    total = jnp.sum(expo, axis=-1, keepdims=True)
    mixed = dot(expo.astype(BF16), v) / total
    if far is not None:
        mixed = [
            jnp.where(far, part[:, 128:], part[:, :128]) for part in (mixed[:size], mixed[size:])
        ]
    else:
        mixed = [mixed[:size], mixed[size:]]
    return jnp.where(low, mixed[0], mixed[1])


def both_ways(far, one, two):
    return jnp.concatenate([jnp.where(far, two, one), jnp.where(far, one, two)], axis=1)


def split_kernel(shift_ref, tok_ref, keep_ref, send_ref, go_ref, back_ref, table_ref):
    core = lax.axis_index("lon") % 2
    a = shift_ref[0, 0]
    for n in range(2):
        for m in range(3):
            table_ref[n, m] = shift_ref[n, m]
    c = shift_ref[0, 2]
    go_ref[0] = c
    few = jnp.where(is_wide(c), 0, jnp.where(c <= FEW, c, c - (WIN_LON - 2 * FEW - 1)))
    back_ref[0] = few + jnp.where(a == shift_ref[1, 0], 0, 2 * FEW + 1)
    for target, out_ref in ((1 - core, send_ref), (core, keep_ref)):
        for slot in range(2):
            level = level_of(target, slot, a)
            for col in range(out_ref.shape[0]):
                out_ref[col, slot] = tok_ref[level, col]


def by_window(columns, scr):
    cols, slots = len(columns), 2
    unit = slots * cols
    size = WIN_LAT * unit
    for col, read in enumerate(columns):
        for slot in range(slots):
            put(scr, size + slot * cols + col, read(slot), unit)
    put(scr, 0, take(scr, scr.shape[1] - size, size))


def reader(ref, col):
    return lambda slot: ref[col, slot].astype(F32)


def ahead_kernel(weight_hbm, gain_hbm, weight_ref, gain_ref, sems):
    loads = [
        pltpu.make_async_copy(weight_hbm, weight_ref, sems.at[0]),
        pltpu.make_async_copy(gain_hbm, gain_ref, sems.at[1]),
    ]
    for load in loads:
        load.start()
    for load in loads:
        load.wait()


def own_kernel(shift_ref, x_ref, gain_ref, qkv_ref, xw_ref, out_ref, xs):
    cols, slots, rows, _ = x_ref.shape
    unit = slots * cols
    size = WIN_LAT * unit
    b = shift_ref[0, 1]
    by_window([reader(x_ref, col) for col in range(cols)], xs)
    gain = gain_ref[...]

    @pl.loop(0, rows // WIN_LAT)
    def _(j):
        at = pl.ds(pl.multiple_of(j * size, size), size)
        tokens = take(xs, pl.multiple_of(((j + 1) * WIN_LAT - b) * unit, 8), size)
        xw_ref[at, :] = tokens.astype(BF16)
        normed = layer_norm(tokens, gain).astype(BF16)
        out_ref[at, :] = dot(normed, qkv_ref[...]).astype(BF16)


def fine_kernel(
    shift_ref, r_ref, xw_ref, qkv, gain_ref, qkv_hbm, proj_hbm,
    out_ref,
    rs, kvr, mix, fr, bias, kv_w, proj_ref, sems,
):
    core = lax.axis_index("lon") % 2
    cols, slots, rows, feats = r_ref.shape
    unit = slots * cols
    wins = rows // WIN_LAT
    size = WIN_LAT * unit
    a, b, c = shift_ref[0, 0], shift_ref[0, 1], shift_ref[0, 2]
    wide = is_wide(c)
    load = pltpu.make_async_copy(proj_hbm, proj_ref, sems.at[1])

    @pl.when(wide)
    def _():
        first = pltpu.make_async_copy(qkv_hbm.at[:, pl.ds(feats, 2 * feats)], kv_w, sems.at[0])
        first.start()
        by_window([reader(r_ref, col) for col in range(cols)], rs)
        gain = gain_ref[...]
        first.wait()
        for j in range(wins):
            tokens = take(rs, pl.multiple_of(((j + 1) * WIN_LAT - b) * unit, 8), size)
            normed = layer_norm(tokens, gain).astype(BF16)
            kvr[pl.ds(j * size, size), :] = dot(normed, kv_w[...]).astype(BF16)

    @pl.when(jnp.logical_not(wide))
    def _():
        kvr[...] = jnp.zeros_like(kvr)

    load.start()

    def parts(index):
        return index // unit, (index // cols) % slots, index % cols

    q_row, q_slot, _ = parts(iota((2 * size, 1), 0) % size)
    k_row, k_slot, _ = parts(iota((1, size), 1))
    far = iota((size, 128), 0) % cols + jnp.where(wide, c, 0) >= cols
    apart = jnp.where((a == 0) | (core == 1), 0, 1)
    q_slot, k_slot = q_slot * apart, k_slot * apart
    q_id = q_slot * 2 + jnp.where(q_row < b, 1, 0)
    k_id = k_slot * 2 + jnp.where(k_row < b, 1, 0)
    bias[0] = jnp.where(q_id == k_id, 0.0, NEG)
    bias[1] = jnp.where(q_slot == k_slot, 0.0, NEG)
    scale = (feats // HEADS) ** -0.5

    for j in range(wins):
        at = pl.ds(j * size, size)
        masked = bias[min(j, 1)]
        for pair in range(feats // 128):
            lanes = pl.ds(pair * 128, 128)
            k_lanes = pl.ds(feats + pair * 128, 128)
            v_lanes = pl.ds(2 * feats + pair * 128, 128)
            mix[at, lanes] = head_pair(
                qkv[at, lanes],
                both_ways(far, qkv[at, k_lanes], kvr[at, lanes]),
                both_ways(far, qkv[at, v_lanes], kvr[at, k_lanes]),
                masked,
                scale,
                far,
            ).astype(BF16)

    load.wait()
    for j in range(wins):
        at = pl.ds(j * size, size)
        fine = xw_ref[at, :].astype(F32) + dot(mix[at, :], proj_ref[...])
        for inner in range(WIN_LAT):
            source = j * WIN_LAT + inner - b
            source = jnp.where(source < 0, source + rows, source)
            put(fr, pl.multiple_of(source * unit, 8), fine[inner * unit : (inner + 1) * unit])
    for slot in range(slots):
        for col in range(cols):
            out_ref[col, slot] = take(fr, slot * cols + col, rows, unit).astype(BF16)


def merge_kernel(f_ref, mgain_ref, mw_hbm, keep_ref, send_ref, coarse_ref, fs, mw_ref, sems):
    core = lax.axis_index("lon") % 2
    cols, slots, rows, feats = f_ref.shape
    loads = []
    for k in range(4):
        at = pl.ds(k * feats, feats)
        loads.append(pltpu.make_async_copy(mw_hbm.at[at], mw_ref.at[at], sems.at[k]))
        loads[k].start()
    for col in range(cols):
        put(fs, col * slots * rows, f_ref[col].astype(F32).reshape(slots * rows, feats))
    own_cols = cols // 2
    for col in range(own_cols):
        keep_ref[col] = f_ref[core * own_cols + col]
        send_ref[col] = f_ref[(1 - core) * own_cols + col]
    groups = []
    block = slots * rows // 2
    for q in range(2):
        for p in range(2):
            starts = [col * slots * rows + p for col in range(q, cols, 2)]
            groups.append(jnp.concatenate([take(fs, start, block, 2) for start in starts], axis=0))
    width = 4 * feats
    mean = sum(jnp.sum(piece, axis=-1, keepdims=True) for piece in groups) / width
    groups = [piece - mean for piece in groups]
    spread = sum(jnp.sum(piece * piece, axis=-1, keepdims=True) for piece in groups) / width
    scaling = lax.rsqrt(spread + EPSILON)
    total = jnp.zeros((own_cols * block, mw_ref.shape[1]), F32)
    for k, piece in enumerate(groups):
        lanes = slice(k * feats, (k + 1) * feats)
        merged = (piece * scaling * mgain_ref[:, lanes]).astype(BF16)
        loads[k].wait()
        total = total + dot(merged, mw_ref[lanes, :])
    coarse_ref[...] = total.astype(BF16).reshape(coarse_ref.shape)


def coarse_kernel(
    shift_ref, own_ref, inside_ref, outside_ref, left_ref, right_ref, gain_ref, qkv_ref, proj_ref,
    out_ref, keys, values, bias, mix,
):
    place = lax.axis_index("lon")
    core = place % 2
    own_cols, depth, feats = own_ref.shape
    side = (place // 2) % (WIN_LON // own_cols)
    size = own_cols * depth
    a, b, c = shift_ref[1, 0], shift_ref[1, 1], shift_ref[1, 2]
    gain = gain_ref[...]
    near_cols = own_cols - lax.rem(c, own_cols)
    far = [
        jnp.where(col < near_cols, right_ref[col].astype(F32), left_ref[col].astype(F32))
        for col in range(own_cols)
    ]
    queries = None
    sets = [ref[...].astype(F32).reshape(size, feats) for ref in (own_ref, inside_ref, outside_ref)]
    for n, full in enumerate((*sets, jnp.concatenate(far, axis=0))):
        at = pl.ds(n * size, size)
        normed = layer_norm(full, gain).astype(BF16)
        if n == 0:
            queries = dot(normed, qkv_ref[:, :feats]).astype(BF16)
        keys[at, :] = dot(normed, qkv_ref[:, feats : 2 * feats]).astype(BF16)
        values[at, :] = dot(normed, qkv_ref[:, 2 * feats :]).astype(BF16)

    def ids(index, chips):
        col = index // depth
        slot = (index // (depth // 2)) % 2
        row = index % (depth // 2)
        window = ((side + chips(col) + 2) * own_cols + col + c) // WIN_LON
        apart = jnp.where((a == 0) | (core == 1), 0, slot)
        return (window * 8 + (row + b) // WIN_LAT) * 2 + apart

    chips_off = (
        lambda col: 0,
        lambda col: 1 - 2 * side,
        lambda col: 2 * side - 1,
        lambda col: jnp.where(col < near_cols, 2, -2),
    )
    q_id = ids(iota((2 * size, 1), 0) % size, chips_off[0])
    for n, chips in enumerate(chips_off):
        k_id = ids(iota((1, size), 1), chips)
        bias[:, n * size : (n + 1) * size] = jnp.where(q_id == k_id, 0.0, NEG)
    scale = (feats // HC) ** -0.5
    for pair in range(feats // 128):
        lanes = pl.ds(pair * 128, 128)
        mix[:, lanes] = head_pair(
            queries[:, pair * 128 : (pair + 1) * 128],
            keys[:, lanes],
            values[:, lanes],
            bias[...],
            scale,
        ).astype(BF16)
    out = own_ref[...].astype(F32).reshape(size, feats) + dot(mix[...], proj_ref[...])
    out_ref[...] = out.astype(BF16).reshape(out_ref.shape)


def expand_kernel(
    shift_ref, own_ref, other_ref, fkeep_ref, fother_ref, gain_ref, weight_ref,
    out_ref, ex,
):
    core = lax.axis_index("lon") % 2
    own_cols, units, feats = own_ref.shape
    slots = 2
    rows = 2 * units // slots
    home = own_cols // 2
    blocks = []
    for ref in (own_ref, other_ref):
        for col in range(home):
            blocks.append(ref[core * home + col].astype(F32))
    blocks = jnp.concatenate(blocks, axis=0).astype(BF16)
    gain = gain_ref[...]
    for q in range(2):
        for p in range(2):
            k = 2 * q + p
            piece = layer_norm(dot(blocks, weight_ref[:, k * feats : (k + 1) * feats]), gain)
            for which in range(2):
                for col in range(home):
                    first = (which * home + col) * units
                    put(ex.at[which, 2 * col + q], p, piece[first : first + units], 2)
    for which, (target, f_ref) in enumerate(((core, fkeep_ref), (1 - core, fother_ref))):
        for slot in range(slots):
            level = level_of(target, slot, shift_ref[1, 0])
            for col in range(2 * home):
                add = take(ex.at[which, col], slot * rows, rows)
                out_ref[level, col] = (f_ref[col, slot].astype(F32) + add).astype(BF16)


VMEM_SPEC = pl.BlockSpec(memory_space=pltpu.VMEM)
SMEM_SPEC = pl.BlockSpec(memory_space=pltpu.SMEM)


HBM_SPEC = pl.BlockSpec(memory_space=pltpu.HBM)


def call(kernel, outs, scratch, arrays, limit, cost=None, hbm=()):
    specs = [SMEM_SPEC if one.dtype == jnp.int32 else VMEM_SPEC for one in arrays]
    arrays = list(arrays)
    for n in hbm:
        specs[n] = HBM_SPEC
        arrays[n] = pltpu.with_memory_space_constraint(arrays[n], pltpu.HBM)
    return pl.pallas_call(
        kernel,
        out_shape=outs,
        in_specs=specs,
        out_specs=jax.tree.map(lambda _: VMEM_SPEC, outs),
        scratch_shapes=scratch,
        compiler_params=pltpu.CompilerParams(vmem_limit_bytes=limit << 20),
        cost_estimate=cost,
    )(*arrays)


def local(
    tokens,
    window_shift,
    fine_gain,
    fine_qkv,
    fine_proj,
    merge_gain,
    merge_weight,
    coarse_gain,
    coarse_qkv,
    coarse_proj,
    expand_weight,
    expand_gain,
):
    levels, rows, dev_cols, feats = tokens.shape
    cols = 2 * dev_cols
    slots = 2
    assert levels == 4 and cols == WIN_LON and rows % (2 * WIN_LAT) == 0
    assert lax.axis_size("lon") % 4 == 0 and WIN_LON == 2 * dev_cols
    core = lax.axis_index("lon") % 2
    sds = jax.ShapeDtypeStruct
    viewed = tokens.transpose(0, 2, 1, 3)

    half = sds((dev_cols, slots, rows, feats), BF16)
    vhalf = pltpu.VMEM(half.shape, BF16)
    one = sds((1,), jnp.int32)
    in_hbm = functools.partial(pltpu.with_memory_space_constraint, memory_space=pltpu.HBM)
    keep, send, go, back, table = pl.pallas_call(
        split_kernel,
        name="split",
        out_shape=(vhalf, vhalf, one, one, sds((2, 3), jnp.int32)),
        in_specs=[SMEM_SPEC, VMEM_SPEC],
        out_specs=(VMEM_SPEC, VMEM_SPEC, SMEM_SPEC, SMEM_SPEC, SMEM_SPEC),
        compiler_params=pltpu.CompilerParams(vmem_limit_bytes=4 << 20),
    )(in_hbm(window_shift), in_hbm(viewed))
    other = swapped(send)
    own_w, gain = call(
        ahead_kernel,
        (pltpu.VMEM(fine_qkv.shape, BF16), pltpu.VMEM((1, feats), F32)),
        [pltpu.SemaphoreType.DMA((2,))],
        (fine_qkv, fine_gain.reshape(1, feats)),
        6,
        hbm=(0, 1),
    )
    grid = jnp.concatenate(
        [jnp.where(core == 0, keep, other), jnp.where(core == 0, other, keep)], axis=0
    )
    unit = slots * cols
    tokens_n = rows * unit
    size = WIN_LAT * unit

    channels = merge_weight.shape[1]
    coarse_depth = rows // 2 * slots
    coarse_n = dev_cols * coarse_depth
    coarse_type = sds((dev_cols, coarse_depth, channels), BF16)

    def branch(c):
        def run(grid):
            around = grid
            if c > WIN_LON - 1 - FEW:
                grid = jnp.concatenate([permuted(grid[: cols - c], -2), grid[cols - c :]], axis=0)
            elif 0 < c <= FEW:
                grid = jnp.concatenate([grid[: cols - c], permuted(grid[cols - c :], 2)], axis=0)
            elif c > 0:
                left = permuted(grid[: cols - c], -2)
                right = permuted(grid[cols - c :], 2)
                around = jnp.concatenate([left, right], axis=0)
            own = call(
                own_kernel,
                (pltpu.VMEM((tokens_n, feats), BF16), pltpu.VMEM((tokens_n, 3 * feats), BF16)),
                [chunked(tokens_n + size, feats)],
                (table, grid, gain, own_w),
                OWN_MIB,
                pl.CostEstimate(
                    flops=tokens_n * feats * feats * 6,
                    bytes_accessed=10 * tokens_n * feats,
                    transcendentals=0,
                ),
            )
            return around, *own

        return run

    branches = [branch(c) for c in range(WIN_LON)]
    around, xw, qkv = lax.switch(go.reshape(()), branches, grid)
    fine = call(
        fine_kernel, pltpu.VMEM(grid.shape, BF16),
        [
            chunked(tokens_n + size, feats),
            pltpu.VMEM((tokens_n, 2 * feats), BF16),
            pltpu.VMEM((tokens_n, feats), BF16),
            chunked(tokens_n, feats),
            pltpu.VMEM((2, 2 * size, size), F32),
            pltpu.VMEM((feats, 2 * feats), BF16),
            pltpu.VMEM(fine_proj.shape, BF16),
            pltpu.SemaphoreType.DMA((2,)),
        ],
        (table, around, xw, qkv, gain, fine_qkv, fine_proj),
        FINE_MIB,
        hbm=(5, 6),
    )

    def returned(c, crossed):
        def run(fine):
            first, last = (cols - c, cols) if c > FEW else (0, cols - c)
            held = fine[first:last]
            moved = fine[:first] if c > FEW else fine[last:]
            steps = 2 if c > FEW else -2
            if crossed:
                held = jnp.stack([held[:, 0], swapped(held[:, 1])], axis=1)
            if c == 0:
                return held
            if crossed:
                moved = [permuted(moved[:, 0], steps), permuted(moved[:, 1], steps, 1)]
                moved = jnp.stack(moved, axis=1)
            else:
                moved = permuted(moved, steps)
            return jnp.concatenate([moved, held] if c > FEW else [held, moved], axis=0)

        return run

    few = [*range(FEW + 1), *range(WIN_LON - FEW, WIN_LON)]
    branches = [returned(c, crossed) for crossed in (False, True) for c in few]
    fine = lax.switch(back.reshape(()), branches, fine)
    fine_keep, fine_send, coarse = call(
        merge_kernel, (half, half, coarse_type),
        [
            chunked(tokens_n, feats),
            pltpu.VMEM(merge_weight.shape, BF16),
            pltpu.SemaphoreType.DMA((4,)),
        ],
        (fine, merge_gain.reshape(1, 4 * feats), merge_weight),
        MERGE_MIB,
        hbm=(2,),
    )
    fine_other = swapped(fine_send)
    right = permuted(coarse, -4)
    outside = paired(coarse, False)
    inside = paired(coarse, True)
    left = permuted(coarse, 4)
    coarse_out = call(
        coarse_kernel, coarse_type,
        [
            pltpu.VMEM((4 * coarse_n, channels), BF16),
            pltpu.VMEM((4 * coarse_n, channels), BF16),
            pltpu.VMEM((2 * coarse_n, 4 * coarse_n), F32),
            pltpu.VMEM((coarse_n, channels), BF16),
        ],
        (
            table, coarse, inside, outside, left, right, coarse_gain.reshape(1, channels), coarse_qkv,
            coarse_proj,
        ),
        COARSE_MIB,
    )
    coarse_other = swapped(coarse_out)
    out = call(
        expand_kernel,
        sds(viewed.shape, BF16),
        [
            pltpu.VMEM((2, dev_cols, feats // 128, slots * rows, 128), F32),
        ],
        (
            table, coarse_out, coarse_other, fine_keep, fine_other,
            expand_gain.reshape(1, feats), expand_weight,
        ),
        EXPAND_MIB,
    )
    return out.transpose(0, 2, 1, 3)


def solution(mesh):
    placed = (P("groups", None, "lon", None), P(), P(), P(), P(), P(), P(), P(), P(), P(), P(), P())
    return jax.shard_map(
        local, mesh=mesh, in_specs=placed, out_specs=P("groups", None, "lon", None), check_vma=False
    )
```

```python
import functools

import jax
import jax.numpy as jnp
from jax import lax
from jax.experimental import pallas as pl
from jax.experimental.pallas import tpu as pltpu
from jax.sharding import PartitionSpec as P


HEADS = 8
HC = 8
WIN_LAT = 6
WIN_LON = 12
EPSILON = 1e-05
NEG = -1e30
FEW = 3
MERGE_MIB = 12
OWN_MIB = 8
FINE_MIB = 24
COARSE_MIB = 16
EXPAND_MIB = 16
F32 = jnp.float32
BF16 = jnp.bfloat16


def permuted(value, steps):
    count = lax.axis_size("lon")
    return lax.ppermute(value, "lon", [(s, (s + steps) % count) for s in range(count)])


def swapped(value):
    count = lax.axis_size("lon")
    return lax.ppermute(value, "lon", [(s, s ^ 1) for s in range(count)])


def paired(value, inside):
    count = lax.axis_size("lon")
    steps = [2 if (s // 2 % 2 == 0) == inside else -2 for s in range(count)]
    return lax.ppermute(value, "lon", [(s, (s + steps[s]) % count) for s in range(count)])


def layer_norm(x, gain):
    center = x - jnp.mean(x, axis=-1, keepdims=True)
    spread = jnp.mean(center * center, axis=-1, keepdims=True)
    return center * lax.rsqrt(spread + EPSILON) * gain


def dot(a, b):
    return jnp.dot(a, b, preferred_element_type=F32)


def dot_t(a, b):
    return lax.dot_general(a, b, (((1,), (1,)), ((), ())), preferred_element_type=F32)


def level_of(core, slot, a):
    if slot == 0:
        return 2 * core
    return jnp.where(core == 0, 1 + 2 * a, 3 - 2 * a)


def is_wide(c):
    return (c > FEW) & (c < WIN_LON - FEW)


def iota(shape, axis):
    return lax.broadcasted_iota(jnp.int32, shape, axis)


def take(ref, start, count, stride=1):
    at = pl.ds(start, count, stride=stride) if stride > 1 else pl.ds(start, count)
    return jnp.concatenate([ref[k, at, :] for k in range(ref.shape[0])], axis=1)


def put(ref, start, value, stride=1):
    at = pl.ds(start, value.shape[0], stride=stride) if stride > 1 else pl.ds(start, value.shape[0])
    for k in range(ref.shape[0]):
        ref[k, at, :] = value[:, k * 128 : (k + 1) * 128]


def chunked(count, width):
    return pltpu.VMEM((width // 128, count, 128), F32)


def head_pair(q, k, v, bias, scale, far=None):
    size = q.shape[0]
    low = iota(q.shape, 1) < 64
    zero = jnp.zeros_like(q)
    q2 = [jnp.where(low, q, zero), jnp.where(low, zero, q)]
    if far is not None:
        q2 = [
            jnp.concatenate([jnp.where(far, zero, one), jnp.where(far, one, zero)], axis=1)
            for one in q2
        ]
    scores = dot_t(jnp.concatenate(q2, axis=0), k) + bias
    top = jnp.max(scores, axis=-1, keepdims=True)
    expo = jnp.exp((scores - top) * scale)
    total = jnp.sum(expo, axis=-1, keepdims=True)
    mixed = dot(expo.astype(BF16), v) / total
    if far is not None:
        mixed = [
            jnp.where(far, part[:, 128:], part[:, :128]) for part in (mixed[:size], mixed[size:])
        ]
    else:
        mixed = [mixed[:size], mixed[size:]]
    return jnp.where(low, mixed[0], mixed[1])


def both_ways(far, one, two):
    return jnp.concatenate([jnp.where(far, two, one), jnp.where(far, one, two)], axis=1)


def split_kernel(shift_ref, tok_ref, keep_ref, send_ref, go_ref, back_ref, table_ref):
    core = lax.axis_index("lon") % 2
    a = shift_ref[0, 0]
    for n in range(2):
        for m in range(3):
            table_ref[n, m] = shift_ref[n, m]
    c = shift_ref[0, 2]
    go_ref[0] = c
    few = jnp.where(is_wide(c), 0, jnp.where(c <= FEW, c, c - (WIN_LON - 2 * FEW - 1)))
    back_ref[0] = few + jnp.where(a == shift_ref[1, 0], 0, 2 * FEW + 1)
    for target, out_ref in ((1 - core, send_ref), (core, keep_ref)):
        for slot in range(2):
            level = level_of(target, slot, a)
            for col in range(out_ref.shape[0]):
                out_ref[col, slot] = tok_ref[level, col]


def by_window(columns, scr):
    cols, slots = len(columns), 2
    unit = slots * cols
    size = WIN_LAT * unit
    for col, read in enumerate(columns):
        for slot in range(slots):
            put(scr, size + slot * cols + col, read(slot), unit)
    put(scr, 0, take(scr, scr.shape[1] - size, size))


def reader(ref, col):
    return lambda slot: ref[col, slot].astype(F32)


def ahead_kernel(weight_hbm, gain_hbm, weight_ref, gain_ref, sems):
    loads = [
        pltpu.make_async_copy(weight_hbm, weight_ref, sems.at[0]),
        pltpu.make_async_copy(gain_hbm, gain_ref, sems.at[1]),
    ]
    for load in loads:
        load.start()
    for load in loads:
        load.wait()


def own_kernel(shift_ref, x_ref, gain_ref, qkv_ref, xw_ref, out_ref, xs, *, unroll):
    cols, slots, rows, _ = x_ref.shape
    unit = slots * cols
    size = WIN_LAT * unit
    b = shift_ref[0, 1]
    by_window([reader(x_ref, col) for col in range(cols)], xs)
    gain = gain_ref[...]

    @pl.loop(0, rows // WIN_LAT, unroll=unroll)
    def _(j):
        at = pl.ds(pl.multiple_of(j * size, size), size)
        tokens = take(xs, pl.multiple_of(((j + 1) * WIN_LAT - b) * unit, 8), size)
        xw_ref[at, :] = tokens.astype(BF16)
        normed = layer_norm(tokens, gain).astype(BF16)
        out_ref[at, :] = dot(normed, qkv_ref[...]).astype(BF16)


def fine_kernel(
    shift_ref, r_ref, xw_ref, qkv, gain_ref, qkv_hbm, proj_hbm,
    out_ref,
    rs, kvr, mix, fr, bias, kv_w, proj_ref, sems,
):
    core = lax.axis_index("lon") % 2
    cols, slots, rows, feats = r_ref.shape
    unit = slots * cols
    wins = rows // WIN_LAT
    size = WIN_LAT * unit
    a, b, c = shift_ref[0, 0], shift_ref[0, 1], shift_ref[0, 2]
    wide = is_wide(c)
    load = pltpu.make_async_copy(proj_hbm, proj_ref, sems.at[1])

    @pl.when(wide)
    def _():
        first = pltpu.make_async_copy(qkv_hbm.at[:, pl.ds(feats, 2 * feats)], kv_w, sems.at[0])
        first.start()
        by_window([reader(r_ref, col) for col in range(cols)], rs)
        gain = gain_ref[...]
        first.wait()
        for j in range(wins):
            tokens = take(rs, pl.multiple_of(((j + 1) * WIN_LAT - b) * unit, 8), size)
            normed = layer_norm(tokens, gain).astype(BF16)
            kvr[pl.ds(j * size, size), :] = dot(normed, kv_w[...]).astype(BF16)

    @pl.when(jnp.logical_not(wide))
    def _():
        kvr[...] = jnp.zeros_like(kvr)

    load.start()

    def parts(index):
        return index // unit, (index // cols) % slots, index % cols

    q_row, q_slot, _ = parts(iota((2 * size, 1), 0) % size)
    k_row, k_slot, _ = parts(iota((1, size), 1))
    far = iota((size, 128), 0) % cols + jnp.where(wide, c, 0) >= cols
    apart = jnp.where((a == 0) | (core == 1), 0, 1)
    q_slot, k_slot = q_slot * apart, k_slot * apart
    q_id = q_slot * 2 + jnp.where(q_row < b, 1, 0)
    k_id = k_slot * 2 + jnp.where(k_row < b, 1, 0)
    bias[0] = jnp.where(q_id == k_id, 0.0, NEG)
    bias[1] = jnp.where(q_slot == k_slot, 0.0, NEG)
    scale = (feats // HEADS) ** -0.5

    for j in range(wins):
        at = pl.ds(j * size, size)
        masked = bias[min(j, 1)]
        for pair in range(feats // 128):
            lanes = pl.ds(pair * 128, 128)
            k_lanes = pl.ds(feats + pair * 128, 128)
            v_lanes = pl.ds(2 * feats + pair * 128, 128)
            mix[at, lanes] = head_pair(
                qkv[at, lanes],
                both_ways(far, qkv[at, k_lanes], kvr[at, lanes]),
                both_ways(far, qkv[at, v_lanes], kvr[at, k_lanes]),
                masked,
                scale,
                far,
            ).astype(BF16)

    load.wait()
    for j in range(wins):
        at = pl.ds(j * size, size)
        fine = xw_ref[at, :].astype(F32) + dot(mix[at, :], proj_ref[...])
        for inner in range(WIN_LAT):
            source = j * WIN_LAT + inner - b
            source = jnp.where(source < 0, source + rows, source)
            put(fr, pl.multiple_of(source * unit, 8), fine[inner * unit : (inner + 1) * unit])
    for slot in range(slots):
        for col in range(cols):
            out_ref[col, slot] = take(fr, slot * cols + col, rows, unit).astype(BF16)


def merge_kernel(f_ref, mgain_ref, mw_hbm, keep_ref, send_ref, coarse_ref, fs, mw_ref, sems):
    core = lax.axis_index("lon") % 2
    cols, slots, rows, feats = f_ref.shape
    loads = []
    for k in range(4):
        at = pl.ds(k * feats, feats)
        loads.append(pltpu.make_async_copy(mw_hbm.at[at], mw_ref.at[at], sems.at[k]))
        loads[k].start()
    for col in range(cols):
        put(fs, col * slots * rows, f_ref[col].astype(F32).reshape(slots * rows, feats))
    own_cols = cols // 2
    for col in range(own_cols):
        keep_ref[col] = f_ref[core * own_cols + col]
        send_ref[col] = f_ref[(1 - core) * own_cols + col]
    groups = []
    block = slots * rows // 2
    for q in range(2):
        for p in range(2):
            starts = [col * slots * rows + p for col in range(q, cols, 2)]
            groups.append(jnp.concatenate([take(fs, start, block, 2) for start in starts], axis=0))
    width = 4 * feats
    mean = sum(jnp.sum(piece, axis=-1, keepdims=True) for piece in groups) / width
    groups = [piece - mean for piece in groups]
    spread = sum(jnp.sum(piece * piece, axis=-1, keepdims=True) for piece in groups) / width
    scaling = lax.rsqrt(spread + EPSILON)
    total = jnp.zeros((own_cols * block, mw_ref.shape[1]), F32)
    for k, piece in enumerate(groups):
        lanes = slice(k * feats, (k + 1) * feats)
        merged = (piece * scaling * mgain_ref[:, lanes]).astype(BF16)
        loads[k].wait()
        total = total + dot(merged, mw_ref[lanes, :])
    coarse_ref[...] = total.astype(BF16).reshape(coarse_ref.shape)


def coarse_kernel(
    shift_ref, own_ref, inside_ref, outside_ref, left_ref, right_ref, gain_ref, qkv_ref, proj_ref,
    out_ref, keys, values, bias, mix,
):
    place = lax.axis_index("lon")
    core = place % 2
    own_cols, depth, feats = own_ref.shape
    side = (place // 2) % (WIN_LON // own_cols)
    size = own_cols * depth
    a, b, c = shift_ref[1, 0], shift_ref[1, 1], shift_ref[1, 2]
    gain = gain_ref[...]
    near_cols = own_cols - lax.rem(c, own_cols)
    far = [
        jnp.where(col < near_cols, right_ref[col].astype(F32), left_ref[col].astype(F32))
        for col in range(own_cols)
    ]
    queries = None
    sets = [ref[...].astype(F32).reshape(size, feats) for ref in (own_ref, inside_ref, outside_ref)]
    for n, full in enumerate((*sets, jnp.concatenate(far, axis=0))):
        at = pl.ds(n * size, size)
        normed = layer_norm(full, gain).astype(BF16)
        if n == 0:
            queries = dot(normed, qkv_ref[:, :feats]).astype(BF16)
        keys[at, :] = dot(normed, qkv_ref[:, feats : 2 * feats]).astype(BF16)
        values[at, :] = dot(normed, qkv_ref[:, 2 * feats :]).astype(BF16)

    def ids(index, chips):
        col = index // depth
        slot = (index // (depth // 2)) % 2
        row = index % (depth // 2)
        window = ((side + chips(col) + 2) * own_cols + col + c) // WIN_LON
        apart = jnp.where((a == 0) | (core == 1), 0, slot)
        return (window * 8 + (row + b) // WIN_LAT) * 2 + apart

    chips_off = (
        lambda col: 0,
        lambda col: 1 - 2 * side,
        lambda col: 2 * side - 1,
        lambda col: jnp.where(col < near_cols, 2, -2),
    )
    q_id = ids(iota((2 * size, 1), 0) % size, chips_off[0])
    for n, chips in enumerate(chips_off):
        k_id = ids(iota((1, size), 1), chips)
        bias[:, n * size : (n + 1) * size] = jnp.where(q_id == k_id, 0.0, NEG)
    scale = (feats // HC) ** -0.5
    for pair in range(feats // 128):
        lanes = pl.ds(pair * 128, 128)
        mix[:, lanes] = head_pair(
            queries[:, pair * 128 : (pair + 1) * 128],
            keys[:, lanes],
            values[:, lanes],
            bias[...],
            scale,
        ).astype(BF16)
    out = own_ref[...].astype(F32).reshape(size, feats) + dot(mix[...], proj_ref[...])
    out_ref[...] = out.astype(BF16).reshape(out_ref.shape)


def expand_kernel(
    shift_ref, own_ref, other_ref, fkeep_ref, fother_ref, gain_ref, weight_ref,
    out_ref, ex,
):
    core = lax.axis_index("lon") % 2
    own_cols, units, feats = own_ref.shape
    slots = 2
    rows = 2 * units // slots
    home = own_cols // 2
    blocks = []
    for ref in (own_ref, other_ref):
        for col in range(home):
            blocks.append(ref[core * home + col].astype(F32))
    blocks = jnp.concatenate(blocks, axis=0).astype(BF16)
    gain = gain_ref[...]
    for q in range(2):
        for p in range(2):
            k = 2 * q + p
            piece = layer_norm(dot(blocks, weight_ref[:, k * feats : (k + 1) * feats]), gain)
            for which in range(2):
                for col in range(home):
                    first = (which * home + col) * units
                    put(ex.at[which, 2 * col + q], p, piece[first : first + units], 2)
    for which, (target, f_ref) in enumerate(((core, fkeep_ref), (1 - core, fother_ref))):
        for slot in range(slots):
            level = level_of(target, slot, shift_ref[1, 0])
            for col in range(2 * home):
                add = take(ex.at[which, col], slot * rows, rows)
                out_ref[level, col] = (f_ref[col, slot].astype(F32) + add).astype(BF16)


VMEM_SPEC = pl.BlockSpec(memory_space=pltpu.VMEM)
SMEM_SPEC = pl.BlockSpec(memory_space=pltpu.SMEM)


HBM_SPEC = pl.BlockSpec(memory_space=pltpu.HBM)


def call(kernel, outs, scratch, arrays, limit, cost=None, hbm=()):
    specs = [SMEM_SPEC if one.dtype == jnp.int32 else VMEM_SPEC for one in arrays]
    arrays = list(arrays)
    for n in hbm:
        specs[n] = HBM_SPEC
        arrays[n] = pltpu.with_memory_space_constraint(arrays[n], pltpu.HBM)
    return pl.pallas_call(
        kernel,
        out_shape=outs,
        in_specs=specs,
        out_specs=jax.tree.map(lambda _: VMEM_SPEC, outs),
        scratch_shapes=scratch,
        compiler_params=pltpu.CompilerParams(vmem_limit_bytes=limit << 20),
        cost_estimate=cost,
    )(*arrays)


def local(
    tokens,
    window_shift,
    fine_gain,
    fine_qkv,
    fine_proj,
    merge_gain,
    merge_weight,
    coarse_gain,
    coarse_qkv,
    coarse_proj,
    expand_weight,
    expand_gain,
):
    levels, rows, dev_cols, feats = tokens.shape
    cols = 2 * dev_cols
    slots = 2
    assert levels == 4 and cols == WIN_LON and rows % (2 * WIN_LAT) == 0
    assert lax.axis_size("lon") % 4 == 0 and WIN_LON == 2 * dev_cols
    core = lax.axis_index("lon") % 2
    sds = jax.ShapeDtypeStruct
    viewed = tokens.transpose(0, 2, 1, 3)

    half = sds((dev_cols, slots, rows, feats), BF16)
    vhalf = pltpu.VMEM(half.shape, BF16)
    one = sds((1,), jnp.int32)
    in_hbm = functools.partial(pltpu.with_memory_space_constraint, memory_space=pltpu.HBM)
    keep, send, go, back, table = pl.pallas_call(
        split_kernel,
        name="split",
        out_shape=(vhalf, vhalf, one, one, sds((2, 3), jnp.int32)),
        in_specs=[SMEM_SPEC, VMEM_SPEC],
        out_specs=(VMEM_SPEC, VMEM_SPEC, SMEM_SPEC, SMEM_SPEC, SMEM_SPEC),
        compiler_params=pltpu.CompilerParams(vmem_limit_bytes=4 << 20),
    )(in_hbm(window_shift), in_hbm(viewed))
    other = swapped(send)
    own_w, gain = call(
        ahead_kernel,
        (pltpu.VMEM(fine_qkv.shape, BF16), pltpu.VMEM((1, feats), F32)),
        [pltpu.SemaphoreType.DMA((2,))],
        (fine_qkv, fine_gain.reshape(1, feats)),
        6,
        hbm=(0, 1),
    )
    grid = jnp.concatenate(
        [jnp.where(core == 0, keep, other), jnp.where(core == 0, other, keep)], axis=0
    )
    unit = slots * cols
    tokens_n = rows * unit
    size = WIN_LAT * unit

    channels = merge_weight.shape[1]
    coarse_depth = rows // 2 * slots
    coarse_n = dev_cols * coarse_depth
    coarse_type = sds((dev_cols, coarse_depth, channels), BF16)

    def branch(c):
        def run(grid):
            around = grid
            if c > WIN_LON - 1 - FEW:
                grid = jnp.concatenate([permuted(grid[: cols - c], -2), grid[cols - c :]], axis=0)
            elif 0 < c <= FEW:
                grid = jnp.concatenate([grid[: cols - c], permuted(grid[cols - c :], 2)], axis=0)
            elif c > 0:
                left = permuted(grid[: cols - c], -2)
                right = permuted(grid[cols - c :], 2)
                around = jnp.concatenate([left, right], axis=0)
            own = call(
                functools.partial(own_kernel, unroll=not FEW < c < WIN_LON - FEW),
                (pltpu.VMEM((tokens_n, feats), BF16), pltpu.VMEM((tokens_n, 3 * feats), BF16)),
                [chunked(tokens_n + size, feats)],
                (table, grid, gain, own_w),
                OWN_MIB,
                pl.CostEstimate(
                    flops=tokens_n * feats * feats * 6,
                    bytes_accessed=10 * tokens_n * feats,
                    transcendentals=0,
                ),
            )
            return around, *own

        return run

    branches = [branch(c) for c in range(WIN_LON)]
    around, xw, qkv = lax.switch(go.reshape(()), branches, grid)
    fine = call(
        fine_kernel, pltpu.VMEM(grid.shape, BF16),
        [
            chunked(tokens_n + size, feats),
            pltpu.VMEM((tokens_n, 2 * feats), BF16),
            pltpu.VMEM((tokens_n, feats), BF16),
            chunked(tokens_n, feats),
            pltpu.VMEM((2, 2 * size, size), F32),
            pltpu.VMEM((feats, 2 * feats), BF16),
            pltpu.VMEM(fine_proj.shape, BF16),
            pltpu.SemaphoreType.DMA((2,)),
        ],
        (table, around, xw, qkv, gain, fine_qkv, fine_proj),
        FINE_MIB,
        hbm=(5, 6),
    )

    def returned(c, crossed):
        def run(fine):
            if c > FEW:
                fine = jnp.concatenate([permuted(fine[: cols - c], 2), fine[cols - c :]], axis=0)
            elif c > 0:
                fine = jnp.concatenate([fine[: cols - c], permuted(fine[cols - c :], -2)], axis=0)
            if crossed:
                fine = jnp.stack([fine[:, 0], swapped(fine[:, 1])], axis=1)
            return fine

        return run

    few = [*range(FEW + 1), *range(WIN_LON - FEW, WIN_LON)]
    branches = [returned(c, crossed) for crossed in (False, True) for c in few]
    fine = lax.switch(back.reshape(()), branches, fine)
    fine_keep, fine_send, coarse = call(
        merge_kernel, (half, half, coarse_type),
        [
            chunked(tokens_n, feats),
            pltpu.VMEM(merge_weight.shape, BF16),
            pltpu.SemaphoreType.DMA((4,)),
        ],
        (fine, merge_gain.reshape(1, 4 * feats), merge_weight),
        MERGE_MIB,
        hbm=(2,),
    )
    fine_other = swapped(fine_send)
    right = permuted(coarse, -4)
    outside = paired(coarse, False)
    inside = paired(coarse, True)
    left = permuted(coarse, 4)
    coarse_out = call(
        coarse_kernel, coarse_type,
        [
            pltpu.VMEM((4 * coarse_n, channels), BF16),
            pltpu.VMEM((4 * coarse_n, channels), BF16),
            pltpu.VMEM((2 * coarse_n, 4 * coarse_n), F32),
            pltpu.VMEM((coarse_n, channels), BF16),
        ],
        (
            table, coarse, inside, outside, left, right, coarse_gain.reshape(1, channels), coarse_qkv,
            coarse_proj,
        ),
        COARSE_MIB,
    )
    coarse_other = swapped(coarse_out)
    out = call(
        expand_kernel,
        sds(viewed.shape, BF16),
        [
            pltpu.VMEM((2, dev_cols, feats // 128, slots * rows, 128), F32),
        ],
        (
            table, coarse_out, coarse_other, fine_keep, fine_other,
            expand_gain.reshape(1, feats), expand_weight,
        ),
        EXPAND_MIB,
    )
    return out.transpose(0, 2, 1, 3)


def solution(mesh):
    placed = (P("groups", None, "lon", None), P(), P(), P(), P(), P(), P(), P(), P(), P(), P(), P())
    return jax.shard_map(
        local, mesh=mesh, in_specs=placed, out_specs=P("groups", None, "lon", None), check_vma=False
    )
```
